256 devices in a mesh: state: 32 (over z_lo, y, core), det: 8 (over x, z_hi).
Axes of the slice: x: 4, y: 4, z: 8 (z_hi: 2, z_lo: 4; z = z_hi * 4 + z_lo), core: 2. Of those that a mesh axis runs over, the one named last changes fastest.
Arguments:
- amplitudes: bfloat16 [128, 16384, 324], P('state', 'det'), may hold values from -0.046875 to 0.046875
Outputs:
- density_tiles: float32 [2, 512, 324, 324], P(None, ('state', 'det'))
The draws below stay inside these ranges and needn't reach their ends.
All inputs are finite; a program needn't handle non-finite values.
Results may differ from the reference program's by a relative error of at most 0.0003.
Values may be sent and summed in bfloat16 or wider, within the bound.
A program may use at most 128 MiB of HBM per device.

```python
import jax
import jax.numpy as jnp
from jax import lax

NOP = 324
ST_DEV = 4
BLOCKS = 32
STATES = 128
NDET = 16384


def levels(stream_key, extent, shards, smallest, top_value):
    loudness, own = 1.0, jax.random.fold_in(stream_key, 6)
    for axis_at, shards_of in shards:
        steps = jnp.exp(jax.random.uniform(jax.random.fold_in(own, axis_at), (shards_of,), jnp.float32, smallest / len(shards), top_value / len(shards)))
        loudness = loudness * jnp.repeat(steps, extent[axis_at] // shards_of).reshape([-1 if axis == axis_at else 1 for axis in range(len(extent))])
    return loudness


def normal_values(own_key, extent, scale, most, shards=(), kind=jnp.bfloat16):
    result = jax.random.normal(own_key, extent, jnp.float32) * scale
    if len(shards) > 0:
        result = levels(own_key, extent, shards, -0.22, 0.18) * result
    return jnp.clip(result, min=-most, max=most).astype(kind)


def setup_inputs(seed: int = 0) -> dict:
    keys = jax.random.split(jax.random.key(seed), 2)
    amplitudes = normal_values(keys[0], (STATES, NDET, NOP), NDET ** -0.5, 0.046875, ((0, 32), (1, 8)))
    return {"amplitudes": amplitudes}


def reference(amplitudes):
    blocks = amplitudes.reshape(BLOCKS, ST_DEV, NDET, NOP)
    results = []
    for hop in (BLOCKS // 2, 1):
        def meet(index):
            mine = lax.dynamic_index_in_dim(blocks, index, 0, keepdims=False).astype(jnp.float32)
            other = lax.dynamic_index_in_dim(blocks, jnp.bitwise_xor(index, hop).astype(jnp.int32), 0, keepdims=False).astype(jnp.float32)
            tiles = jnp.einsum("adp,bdq->abpq", mine, other, precision=lax.Precision.HIGHEST)
            return tiles.reshape(ST_DEV * ST_DEV, NOP, NOP)
        tiles = lax.map(meet, jnp.arange(BLOCKS, dtype=jnp.int32))
        results.append(tiles.reshape(STATES * ST_DEV, NOP, NOP))
    return jnp.stack(results)
```

```python
import functools

import jax
import jax.numpy as jnp
from jax import lax
from jax.experimental import pallas as pl
from jax.experimental.pallas import tpu as pltpu
from jax.sharding import Mesh, PartitionSpec as P

MESH = pl.DeviceIdType.MESH
ROWS = 336
CHUNK = 112
CHUNKS = 3
HALF = 168
FAR = 2 * CHUNKS


def group_of(a, scheme):
    if scheme == 0:
        return ((a + 1) // 2) % 2, a // 2
    return a // 2, a % 2


def product(left, right):
    return lax.dot_general(left, right, (((1,), (1,)), ((), ())), preferred_element_type=jnp.float32)


class Stream:
    def __init__(self, refs, index, sems, first_sem, scheme, mirror):
        self.t, self.r1, self.r2, self.r3, self.f, self.r4 = (ref.at[index] for ref in refs)
        self.send_sem, self.recv_sem = sems
        self.sem = first_sem
        x, self.zh = lax.axis_index("x"), lax.axis_index("zh")
        self.group, self.member = group_of(x, scheme)
        near, far = {"x": x + 1 - 2 * (x % 2)}, {"x": 3 - x}
        self.partners = (near, far) if scheme == 0 else (far, near)
        self.partners = self.partners + ({"zh": 1 - self.zh}, mirror)

    def copy(self, step):
        source, target = (
            (self.t.at[1 - self.group], self.r1),
            (self.t.at[self.group, 1 - self.member], self.r2),
            (self.t.at[self.group, self.member, 1 - self.zh], self.r3),
            (self.f, self.r4),
        )[step]
        return pltpu.make_async_remote_copy(
            src_ref=source,
            dst_ref=target,
            send_sem=self.send_sem.at[self.sem + step],
            recv_sem=self.recv_sem.at[self.sem + step],
            device_id=self.partners[step],
            device_id_type=MESH,
        )

    def over_x(self):
        self.copy(0).start()

    def over_x_again(self):
        self.copy(0).wait_recv()
        g, m = self.group, self.member
        self.t[g, 1 - m] += self.r1[1 - m]
        self.copy(1).start()
        self.t[g, m] += self.r1[m]

    def over_zh(self):
        self.copy(1).wait_recv()
        g, m, h = self.group, self.member, self.zh
        self.t[g, m, 1 - h] += self.r2[1 - h]
        self.copy(2).start()
        self.t[g, m, h] += self.r2[h]

    def to_mirror(self):
        self.copy(2).wait_recv()
        self.f[...] = self.t[self.group, self.member, self.zh] + self.r3[...]
        self.copy(3).start()

    def finish(self):
        self.copy(3).wait_recv()

    def drain(self):
        for step in range(4):
            self.copy(step).wait_send()


def kernel(
    a_ref, out_ref, own, beside, held,
    t0, r10, r20, r30, f0, r40, t1, r11, r21, r31, f1, r41,
    send_sem, recv_sem, load_sem, ex_send, ex_recv,
):
    zb, core = lax.axis_index("zb"), lax.axis_index("core")
    x, zh = lax.axis_index("x"), lax.axis_index("zh")
    half = own.shape[2] // 2

    def mirror(s, side, name):
        b = 2 * zh + (x + s) % 2
        return {name: 1 - side, "x": b, "zh": x // 2}

    far_mirrors = [mirror(s, zb, "zb") for s in range(2)]
    near_mirror = mirror(core, core, "core")
    partners = [
        {"zb": 1 - zb}, {"core": 1 - core}, {"x": x + 1 - 2 * (x % 2)}, {"x": 3 - x}, {"zh": 1 - zh},
        *far_mirrors, near_mirror,
    ]
    barrier = pltpu.get_barrier_semaphore()
    for partner in partners:
        pl.semaphore_signal(barrier, inc=1, device_id=partner, device_id_type=MESH)
    pl.semaphore_wait(barrier, len(partners))

    here = pl.ds(pl.multiple_of(zb * half, half), half)
    away = pl.ds(pl.multiple_of((1 - zb) * half, half), half)
    load = pltpu.make_async_copy(a_ref, own, load_sem)
    load.start()
    to_side = pltpu.make_async_remote_copy(
        src_ref=a_ref, dst_ref=beside, send_sem=ex_send.at[CHUNKS], recv_sem=ex_recv.at[CHUNKS],
        device_id={"core": 1 - core}, device_id_type=MESH,
    )
    exchange = []
    for c in range(CHUNKS):
        rows = pl.ds(c * CHUNK, CHUNK)
        exchange.append(pltpu.make_async_remote_copy(
            src_ref=a_ref.at[:, rows, away], dst_ref=held.at[:, rows, :],
            send_sem=ex_send.at[c], recv_sem=ex_recv.at[c],
            device_id={"zb": 1 - zb}, device_id_type=MESH,
        ))
    exchange[0].start()
    to_side.start()
    for copy in exchange[1:]:
        copy.start()

    sems = (send_sem, recv_sem)
    far = [
        [
            Stream((t0, r10, r20, r30, f0, r40), 2 * c + s, sems, 4 * (2 * c + s), s, far_mirrors[s])
            for s in range(2)
        ]
        for c in range(CHUNKS)
    ]
    near = [
        Stream((t1, r11, r21, r31, f1, r41), h, sems, 4 * (FAR + h), h, near_mirror) for h in range(2)
    ]

    load.wait()
    to_side.wait_recv()

    @pl.loop(0, 4)
    def _(a):
        parity = (a + core) % 2
        for bh in range(2):
            tile = product(beside[2 * bh + parity], own[a])
            for h in range(2):
                g, m = group_of(a, h)
                t1[h, g, m, bh] = tile[h * HALF:(h + 1) * HALF]

    for stream in near:
        stream.over_x()
    for stream in near:
        stream.over_x_again()

    def multiply(c):
        exchange[c].wait_recv()
        rows = pl.ds(c * CHUNK, CHUNK)

        @pl.loop(0, 4)
        def _(a):
            left = [held[2 * bh + (a + s) % 2, rows, :] for s in range(2) for bh in range(2)]
            tile = product(jnp.concatenate(left, 0), own[a, :, here])
            for s in range(2):
                g, m = group_of(a, s)
                for bh in range(2):
                    at = (2 * s + bh) * CHUNK
                    t0[2 * c + s, g, m, bh] = tile[at:at + CHUNK]

        for stream in far[c]:
            stream.over_x()

    multiply(0)
    for stream in near:
        stream.over_zh()
    for stream in far[0]:
        stream.over_x_again()
    for stream in far[0]:
        stream.over_zh()
    multiply(1)
    for stream in far[1]:
        stream.over_x_again()
    for stream in far[1]:
        stream.over_zh()
    multiply(2)
    for stream in near:
        stream.to_mirror()
    for stream in far[0]:
        stream.to_mirror()
    for stream in far[2]:
        stream.over_x_again()
    for stream in far[2]:
        stream.over_zh()
    for stream in far[1]:
        stream.to_mirror()

    ops = out_ref.shape[2]
    slot = (x + core) % 2
    for h in range(2):
        near[h].finish()
    tile = jnp.concatenate([f1[0], f1[1]], 0).T
    out_ref[1, slot] = tile[:ops, :ops]
    out_ref[1, 1 - slot] = jnp.concatenate([r41[0], r41[1]], 0)[:ops, :ops]
    for stream in far[2]:
        stream.to_mirror()
    for s in range(2):
        for c in range(CHUNKS):
            far[c][s].finish()
        slot = (x + s) % 2
        tile = jnp.concatenate([f0[2 * c + s] for c in range(CHUNKS)], 0).T
        got = jnp.concatenate([r40[2 * c + s] for c in range(CHUNKS)], 0)
        out_ref[0, slot] = tile[:ops, :ops] + got[:ops, :ops]

    to_side.wait_send()
    for copy in exchange:
        copy.wait_send()
    for streams in (*far, near):
        for stream in streams:
            stream.drain()


def buffers(streams, rows):
    lead = [(2, 2, 2), (2, 2), (2,), (), (), ()]
    return [pltpu.VMEM((streams, *shape, rows, ROWS), jnp.float32) for shape in lead]


def on_device(amplitudes):
    states, dets, ops = amplitudes.shape
    block = jnp.pad(amplitudes.transpose(0, 2, 1), ((0, 0), (0, ROWS - ops), (0, 0)))
    dma = pltpu.SemaphoreType.DMA
    return pl.pallas_call(
        kernel,
        out_shape=jax.ShapeDtypeStruct((2, 2, ops, ops), jnp.float32),
        in_specs=[pl.BlockSpec(memory_space=pl.ANY)],
        out_specs=pl.BlockSpec(memory_space=pltpu.VMEM),
        scratch_shapes=[
            pltpu.VMEM((states, ROWS, dets), jnp.bfloat16),
            pltpu.VMEM((states, ROWS, dets), jnp.bfloat16),
            pltpu.VMEM((states, ROWS, dets // 2), jnp.bfloat16),
            *buffers(FAR, CHUNK),
            *buffers(2, HALF),
            dma((4 * (FAR + 2),)),
            dma((4 * (FAR + 2),)),
            dma,
            dma((CHUNKS + 1,)),
            dma((CHUNKS + 1,)),
        ],
        compiler_params=pltpu.CompilerParams(
            collective_id=0, has_side_effects=True, vmem_limit_bytes=64 * 1024 * 1024 - 65536,
        ),
    )(block)


def solution(mesh):
    fine = Mesh(mesh.devices.reshape(2, 2, 4, 2, 4, 2), ("zb", "za", "y", "core", "x", "zh"))
    state, det = ("zb", "za", "y", "core"), ("x", "zh")
    return jax.shard_map(
        on_device,
        mesh=fine,
        in_specs=(P(state, det, None),),
        out_specs=P(None, state + det, None, None),
        check_vma=False,
    )
```

```python
import jax
import jax.numpy as jnp
from jax import lax
from jax.experimental import pallas as pl
from jax.experimental.pallas import tpu as pltpu
from jax.sharding import Mesh, PartitionSpec as P

MESH = pl.DeviceIdType.MESH
ROWS = 336
LANES = 384
CHUNK = 112
CHUNKS = 3
PACKED = 2 * CHUNK + CHUNK // 2 + 8
HOME, AWAY, NEAR = 0, CHUNKS, 2 * CHUNKS
STREAMS = 3 * CHUNKS
STEPS = 4


def group_of(a, scheme):
    if scheme == 0:
        return ((a + 1) // 2) % 2, a // 2
    return a // 2, a % 2


def product(left, right):
    return lax.dot_general(left, right, (((1,), (1,)), ((), ())), preferred_element_type=jnp.float32)


def lanes(rows):
    return lax.broadcasted_iota(jnp.int32, (rows, 128), 1)


def pack(tile):
    third = tile[:, 256:]
    if third.shape[1] < 128:
        third = jnp.concatenate([third, jnp.zeros((CHUNK, 128 - third.shape[1]), jnp.float32)], 1)
    folded = jnp.where(lanes(CHUNK // 2) < 64, third[:CHUNK // 2], pltpu.roll(third[CHUNK // 2:], 64, 1))
    rest = jnp.concatenate([third, jnp.zeros((128 - CHUNK, 128), jnp.float32)], 0).T[64:72]
    return jnp.concatenate([tile[:, :128], tile[:, 128:256], folded, rest], 0)


def unpack(packed):
    folded = packed[2 * CHUNK:PACKED - 8]
    third = jnp.concatenate([folded, pltpu.roll(folded, 64, 1)], 0)
    rest = jnp.concatenate([packed[PACKED - 8:], jnp.zeros((120, 128), jnp.float32)], 0).T[:CHUNK]
    third = jnp.where(lanes(CHUNK) < 64, third, pltpu.roll(rest, 64, 1))
    return jnp.concatenate([packed[:CHUNK], packed[CHUNK:2 * CHUNK], third], 1)


def whole(chunks):
    return jnp.concatenate([unpack(chunk) for chunk in chunks], 0)


def flipped(tile):
    return jnp.concatenate([tile, jnp.zeros((LANES - ROWS, LANES), jnp.float32)], 0).T


def remote(source, target, sends, recvs, send_at, recv_at, device):
    return pltpu.make_async_remote_copy(
        src_ref=source, dst_ref=target, send_sem=sends.at[send_at], recv_sem=recvs.at[recv_at],
        device_id=device, device_id_type=MESH,
    )


class Stream:
    def __init__(self, index, scheme, refs, sems):
        self.t, self.r1, self.r2, self.r3, self.f, self.r4 = (ref.at[index] for ref in refs)
        self.sems, self.sem = sems, STEPS * index
        x, self.zh = lax.axis_index("x"), lax.axis_index("zh")
        self.group, self.member = group_of(x, scheme)
        near, far = {"x": x + 1 - 2 * (x % 2)}, {"x": 3 - x}
        self.first, self.second = (near, far) if scheme == 0 else (far, near)

    def copy(self, step, source, target, device):
        return remote(source, target, *self.sems, self.sem + step, self.sem + step, device)

    def over_x(self):
        self.copy0 = self.copy(0, self.t.at[1 - self.group], self.r1, self.first)
        self.copy0.start()

    def over_x_again(self):
        self.copy0.wait_recv()
        g, m = self.group, self.member
        self.t[g, 1 - m] += self.r1[1 - m]
        self.copy1 = self.copy(1, self.t.at[g, 1 - m], self.r2, self.second)
        self.copy1.start()
        self.t[g, m] += self.r1[m]

    def over_zh(self):
        self.copy1.wait_recv()
        g, m, h = self.group, self.member, self.zh
        self.t[g, m, 1 - h] += self.r2[1 - h]
        self.copy2 = self.copy(2, self.t.at[g, m, 1 - h], self.r3, {"zh": 1 - h})
        self.copy2.start()
        self.t[g, m, h] += self.r2[h]

    def summed(self):
        self.copy2.wait_recv()
        return self.t[self.group, self.member, self.zh] + self.r3[...]

    def to_mirror(self, value, device):
        self.f[...] = value
        self.copy3 = self.copy(3, self.f, self.r4, device)
        self.copy3.start()

    def go_home(self, r5, homes):
        self.copy1.wait_recv()
        g, m = self.group, self.member
        for bh in range(2):
            self.t[g, m, bh] += self.r2[bh]
        self.home_copies = [
            remote(self.t.at[g, m, bh], r5.at[self.zh], *self.sems, self.sem + 2 + bh, self.sem + 2 + self.zh, homes[bh])
            for bh in range(2)
        ]
        for copy in self.home_copies:
            copy.start()
        return [
            remote(self.t.at[g, m, z], r5.at[z], *self.sems, self.sem + 2 + z, self.sem + 2 + z, homes[z])
            for z in range(2)
        ]


def kernel(
    a_ref, out_ref, own, beside, held, t, r1, r2, r3, f, r4, r5,
    send_sem, recv_sem, load_sem, ex_send, ex_recv,
):
    zb, core = lax.axis_index("zb"), lax.axis_index("core")
    x, zh = lax.axis_index("x"), lax.axis_index("zh")
    half = held.shape[2]
    ops, given = out_ref.shape[2], a_ref.shape[1]

    other = {"zb": 1 - zb}
    home_mirror = {**other, "x": 2 * zh + (x + zb) % 2, "zh": x // 2}
    helpers = [{**other, "x": 2 * zh + (x + zb) % 2, "zh": z} for z in range(2)]
    homes = [{**other, "x": 2 * bh + (x + 1 - zb) % 2, "zh": x // 2} for bh in range(2)]
    near_mirror = {"core": 1 - core, "x": 2 * zh + (x + core) % 2, "zh": x // 2}
    partners = [
        other, {"core": 1 - core}, {"x": x + 1 - 2 * (x % 2)}, {"x": 3 - x}, {"zh": 1 - zh},
        *helpers, *homes, near_mirror,
    ]
    barrier = pltpu.get_barrier_semaphore()
    for partner in partners:
        pl.semaphore_signal(barrier, inc=1, device_id=partner, device_id_type=MESH)
    pl.semaphore_wait(barrier, len(partners))

    here = pl.ds(pl.multiple_of(zb * half, half), half)
    away = pl.ds(pl.multiple_of((1 - zb) * half, half), half)
    exchange = []
    for c in range(CHUNKS):
        rows = pl.ds(c * CHUNK, min(CHUNK, given - c * CHUNK))
        exchange.append(
            remote(a_ref.at[:, rows, away], held.at[:, rows, :], ex_send, ex_recv, c, c, other)
        )
        exchange[c].start()
    every = pl.ds(0, given)
    to_side = remote(a_ref, beside.at[:, every, :], ex_send, ex_recv, CHUNKS, CHUNKS, {"core": 1 - core})
    to_side.start()
    load = pltpu.make_async_copy(a_ref, own.at[:, every, :], load_sem)
    load.start()

    refs, sems = (t, r1, r2, r3, f, r4), (send_sem, recv_sem)
    home = [Stream(HOME + c, 0, refs, sems) for c in range(CHUNKS)]
    going = [Stream(AWAY + c, 1, refs, sems) for c in range(CHUNKS)]
    near = [Stream(NEAR + c, c % 2, refs, sems) for c in range(CHUNKS)]

    load.wait()
    to_side.wait_recv()

    @pl.loop(0, 4)
    def _(a):
        for bh in range(2):
            tile = product(beside[2 * bh + (a + core) % 2], own[a])
            for c in range(CHUNKS):
                g, m = group_of(a, c % 2)
                t[NEAR + c, g, m, bh] = pack(tile[c * CHUNK:(c + 1) * CHUNK])

    for stream in near:
        stream.over_x()
    for stream in near:
        stream.over_x_again()

    arrivals = []

    def far_chunk(c, between):
        exchange[c].wait_recv()
        rows = pl.ds(c * CHUNK, CHUNK)

        @pl.loop(0, 4)
        def _(a):
            left = [held[2 * bh + (a + role + zb) % 2, rows, :] for role in range(2) for bh in range(2)]
            tile = product(jnp.concatenate(left, 0), own[a, :, here])
            for role in range(2):
                g, m = group_of(a, role)
                for bh in range(2):
                    start = (2 * role + bh) * CHUNK
                    t[role * AWAY + c, g, m, bh] = pack(tile[start:start + CHUNK])

        home[c].over_x()
        going[c].over_x()
        for stream in between:
            stream.over_zh()
        home[c].over_x_again()
        going[c].over_x_again()
        home[c].over_zh()
        arrivals.append(going[c].go_home(r5.at[c], homes))

    far_chunk(0, near)
    far_chunk(1, ())
    far_chunk(2, ())

    for stream in near:
        stream.to_mirror(stream.summed(), near_mirror)
    slot = (x + core) % 2
    out_ref[1, slot] = flipped(whole([stream.f[...] for stream in near]))[:ops, :ops]

    for c in range(CHUNKS):
        for copy in arrivals[c]:
            copy.wait_recv()
    helped = flipped(whole([r5[c, 0] + r5[c, 1] for c in range(CHUNKS)]))
    for c in range(CHUNKS):
        home[c].to_mirror(home[c].summed() + pack(helped[c * CHUNK:(c + 1) * CHUNK]), home_mirror)
    for stream in near:
        stream.copy3.wait_recv()
    out_ref[1, 1 - slot] = whole([stream.r4[...] for stream in near])[:ops, :ops]
    slot = (x + zb) % 2
    out_ref[0, slot] = flipped(whole([stream.f[...] for stream in home]))[:ops, :ops]
    for stream in home:
        stream.copy3.wait_recv()
    out_ref[0, 1 - slot] = whole([stream.r4[...] for stream in home])[:ops, :ops]

    to_side.wait_send()
    for copy in exchange:
        copy.wait_send()
    for stream in (*home, *near):
        for copy in (stream.copy0, stream.copy1, stream.copy2, stream.copy3):
            copy.wait_send()
    for stream in going:
        for copy in (stream.copy0, stream.copy1, *stream.home_copies):
            copy.wait_send()


def on_device(amplitudes):
    states, dets, ops = amplitudes.shape
    block = jnp.pad(amplitudes.transpose(0, 2, 1), ((0, 0), (0, -ops % 8), (0, 0)))
    dma = pltpu.SemaphoreType.DMA

    def tiles(*lead):
        return pltpu.VMEM((*lead, PACKED, 128), jnp.float32)

    return pl.pallas_call(
        kernel,
        out_shape=jax.ShapeDtypeStruct((2, 2, ops, ops), jnp.float32),
        in_specs=[pl.BlockSpec(memory_space=pl.ANY)],
        out_specs=pl.BlockSpec(memory_space=pltpu.VMEM),
        scratch_shapes=[
            pltpu.VMEM((states, ROWS, dets), jnp.bfloat16),
            pltpu.VMEM((states, ROWS, dets), jnp.bfloat16),
            pltpu.VMEM((states, ROWS, dets // 2), jnp.bfloat16),
            tiles(STREAMS, 2, 2, 2),
            tiles(STREAMS, 2, 2),
            tiles(STREAMS, 2),
            tiles(STREAMS),
            tiles(STREAMS),
            tiles(STREAMS),
            tiles(CHUNKS, 2),
            dma((STREAMS * STEPS,)),
            dma((STREAMS * STEPS,)),
            dma,
            dma((CHUNKS + 1,)),
            dma((CHUNKS + 1,)),
        ],
        compiler_params=pltpu.CompilerParams(
            collective_id=0, has_side_effects=True, vmem_limit_bytes=64 * 1024 * 1024 - 65536,
        ),
    )(block)


def solution(mesh):
    fine = Mesh(mesh.devices.reshape(2, 2, 4, 2, 4, 2), ("zb", "za", "y", "core", "x", "zh"))
    state, det = ("zb", "za", "y", "core"), ("x", "zh")
    return jax.shard_map(
        on_device,
        mesh=fine,
        in_specs=(P(state, det, None),),
        out_specs=P(None, state + det, None, None),
        check_vma=False,
    )
```

```python
import jax
import jax.numpy as jnp
from jax import lax
from jax.experimental import pallas as pl
from jax.experimental.pallas import tpu as pltpu
from jax.sharding import Mesh, PartitionSpec as P

MESH = pl.DeviceIdType.MESH
ROWS = 336
LANES = 384
SIZES = (96, 96, 80, 64)
STARTS = (0, 96, 192, 272)
CHUNKS = len(SIZES)
HOME, AWAY, NEAR = 0, CHUNKS, 2 * CHUNKS
STREAMS = 3 * CHUNKS
STEPS = 4


def group_of(a, scheme):
    if scheme == 0:
        return ((a + 1) // 2) % 2, a // 2
    return a // 2, a % 2


def product(left, right):
    return lax.dot_general(left, right, (((1,), (1,)), ((), ())), preferred_element_type=jnp.float32)


def lanes(rows):
    return lax.broadcasted_iota(jnp.int32, (rows, 128), 1)


def packed_rows(size):
    return 2 * size + size // 2 + 8


def pack(tile):
    size, third = tile.shape[0], tile[:, 256:]
    if third.shape[1] < 128:
        third = jnp.concatenate([third, jnp.zeros((size, 128 - third.shape[1]), jnp.float32)], 1)
    folded = jnp.where(lanes(size // 2) < 64, third[:size // 2], pltpu.roll(third[size // 2:], 64, 1))
    rest = jnp.concatenate([third, jnp.zeros((128 - size, 128), jnp.float32)], 0).T[64:72]
    return jnp.concatenate([tile[:, :128], tile[:, 128:256], folded, rest], 0)


def unpack(packed, size):
    end = packed_rows(size)
    folded = packed[2 * size:end - 8]
    third = jnp.concatenate([folded, pltpu.roll(folded, 64, 1)], 0)
    rest = jnp.concatenate([packed[end - 8:], jnp.zeros((120, 128), jnp.float32)], 0).T[:size]
    third = jnp.where(lanes(size) < 64, third, pltpu.roll(rest, 64, 1))
    return jnp.concatenate([packed[:size], packed[size:2 * size], third], 1)


def whole(chunks):
    return jnp.concatenate([unpack(chunk, size) for chunk, size in zip(chunks, SIZES)], 0)


def flipped(tile):
    return jnp.concatenate([tile, jnp.zeros((LANES - ROWS, LANES), jnp.float32)], 0).T


def remote(source, target, sends, recvs, send_at, recv_at, device):
    return pltpu.make_async_remote_copy(
        src_ref=source, dst_ref=target, send_sem=sends.at[send_at], recv_sem=recvs.at[recv_at],
        device_id=device, device_id_type=MESH,
    )


class Stream:
    def __init__(self, index, scheme, refs, sems):
        rows = pl.ds(0, packed_rows(SIZES[index % CHUNKS]))
        t, r1, r2, r3, f, r4 = refs
        self.t, self.r1 = t.at[index, :, :, :, rows], r1.at[index, :, :, rows]
        self.r2 = r2.at[index, :, rows]
        self.r3, self.f, self.r4 = (ref.at[index, rows] for ref in (r3, f, r4))
        self.sems, self.sem = sems, STEPS * index
        x, self.zh = lax.axis_index("x"), lax.axis_index("zh")
        self.group, self.member = group_of(x, scheme)
        near, far = {"x": x + 1 - 2 * (x % 2)}, {"x": 3 - x}
        self.first, self.second = (near, far) if scheme == 0 else (far, near)

    def copy(self, step, source, target, device):
        return remote(source, target, *self.sems, self.sem + step, self.sem + step, device)

    def over_x(self):
        self.copy0 = self.copy(0, self.t.at[1 - self.group], self.r1, self.first)
        self.copy0.start()

    def over_x_again(self):
        self.copy0.wait_recv()
        g, m = self.group, self.member
        self.t[g, 1 - m] += self.r1[1 - m]
        self.copy1 = self.copy(1, self.t.at[g, 1 - m], self.r2, self.second)
        self.copy1.start()
        self.t[g, m] += self.r1[m]

    def over_zh(self):
        self.copy1.wait_recv()
        g, m, h = self.group, self.member, self.zh
        self.t[g, m, 1 - h] += self.r2[1 - h]
        self.copy2 = self.copy(2, self.t.at[g, m, 1 - h], self.r3, {"zh": 1 - h})
        self.copy2.start()
        self.t[g, m, h] += self.r2[h]

    def summed(self):
        self.copy2.wait_recv()
        return self.t[self.group, self.member, self.zh] + self.r3[...]

    def to_mirror(self, value, device):
        self.f[...] = value
        self.copy3 = self.copy(3, self.f, self.r4, device)
        self.copy3.start()

    def go_home(self, r5, homes):
        self.copy1.wait_recv()
        g, m = self.group, self.member
        for bh in range(2):
            self.t[g, m, bh] += self.r2[bh]
        self.home_copies = [
            remote(self.t.at[g, m, bh], r5.at[self.zh], *self.sems, self.sem + 2 + bh, self.sem + 2 + self.zh, homes[bh])
            for bh in range(2)
        ]
        for copy in self.home_copies:
            copy.start()
        return [
            remote(self.t.at[g, m, z], r5.at[z], *self.sems, self.sem + 2 + z, self.sem + 2 + z, homes[z])
            for z in range(2)
        ]


def kernel(
    a_ref, out_ref, own, beside, held, t, r1, r2, r3, f, r4, r5,
    send_sem, recv_sem, load_sem, ex_send, ex_recv,
):
    zb, core = lax.axis_index("zb"), lax.axis_index("core")
    x, zh = lax.axis_index("x"), lax.axis_index("zh")
    half = held.shape[2]
    ops, given = out_ref.shape[2], a_ref.shape[1]

    other = {"zb": 1 - zb}
    home_mirror = {**other, "x": 2 * zh + (x + zb) % 2, "zh": x // 2}
    from_mirror = {**other, "x": 2 * zh + (x + 1 - zb) % 2, "zh": x // 2}
    homes = [{**other, "zh": z} for z in range(2)]
    near_mirror = {"core": 1 - core, "x": 2 * zh + (x + core) % 2, "zh": x // 2}
    partners = [
        {"core": 1 - core}, {"x": x + 1 - 2 * (x % 2)}, {"x": 3 - x}, {"zh": 1 - zh},
        *homes, home_mirror, from_mirror, near_mirror,
    ]
    barrier = pltpu.get_barrier_semaphore()
    for partner in partners:
        pl.semaphore_signal(barrier, inc=1, device_id=partner, device_id_type=MESH)
    pl.semaphore_wait(barrier, len(partners))

    here = pl.ds(pl.multiple_of(zb * half, half), half)
    away = pl.ds(pl.multiple_of((1 - zb) * half, half), half)
    exchange = []
    for c in range(CHUNKS):
        rows = pl.ds(STARTS[c], min(SIZES[c], given - STARTS[c]))
        exchange.append(
            remote(a_ref.at[:, rows, away], held.at[:, rows, :], ex_send, ex_recv, c, c, other)
        )
    for copy in exchange[:-1]:
        copy.start()
    every = pl.ds(0, given)
    to_side = remote(a_ref, beside.at[:, every, :], ex_send, ex_recv, CHUNKS, CHUNKS, {"core": 1 - core})
    to_side.start()
    load = pltpu.make_async_copy(a_ref, own.at[:, every, :], load_sem)
    load.start()

    refs, sems = (t, r1, r2, r3, f, r4), (send_sem, recv_sem)
    home = [Stream(HOME + c, 0, refs, sems) for c in range(CHUNKS)]
    going = [Stream(AWAY + c, 1, refs, sems) for c in range(CHUNKS)]
    near = [Stream(NEAR + c, c % 2, refs, sems) for c in range(CHUNKS)]

    load.wait()
    to_side.wait_recv()

    @pl.loop(0, 4)
    def _(a):
        for bh in range(2):
            tile = product(beside[2 * bh + (a + core) % 2], own[a])
            for c in range(CHUNKS):
                g, m = group_of(a, c % 2)
                near[c].t[g, m, bh] = pack(tile[STARTS[c]:STARTS[c] + SIZES[c]])

    for stream in near:
        stream.over_x()
    for stream in near:
        stream.over_x_again()

    arrivals = []

    def far_chunk(c):
        exchange[c].wait_recv()
        rows, size = pl.ds(STARTS[c], SIZES[c]), SIZES[c]

        @pl.loop(0, 4)
        def _(a):
            left = [held[2 * bh + (a + role + zb) % 2, rows, :] for role in range(2) for bh in range(2)]
            tile = product(jnp.concatenate(left, 0), own[a, :, here])
            g, m = group_of(a, 0)
            for bh in range(2):
                home[c].t[g, m, bh] = pack(tile[bh * size:(bh + 1) * size])
                going[c].t[bh, (a + 1 + zb) % 2, a // 2] = pack(tile[(2 + bh) * size:(3 + bh) * size])

        home[c].over_x()
        going[c].over_x()
        if c == 0:
            for stream in near:
                stream.over_zh()
            exchange[-1].start()
        home[c].over_x_again()
        going[c].over_x_again()
        home[c].over_zh()
        arrivals.append(going[c].go_home(r5.at[c, :, pl.ds(0, packed_rows(size))], homes))

    for c in range(CHUNKS):
        far_chunk(c)

    for stream in near:
        stream.to_mirror(stream.summed(), near_mirror)
    slot = (x + core) % 2
    out_ref[1, slot] = flipped(whole([stream.f[...] for stream in near]))[:ops, :ops]

    for c in range(CHUNKS):
        for copy in arrivals[c]:
            copy.wait_recv()
    ends = [packed_rows(size) for size in SIZES]
    helped = flipped(whole([r5[c, 0, :ends[c]] + r5[c, 1, :ends[c]] for c in range(CHUNKS)]))
    for c in range(CHUNKS):
        part = helped[STARTS[c]:STARTS[c] + SIZES[c]]
        home[c].to_mirror(home[c].summed() + pack(part), home_mirror)
    for stream in near:
        stream.copy3.wait_recv()
    out_ref[1, 1 - slot] = whole([stream.r4[...] for stream in near])[:ops, :ops]
    slot = (x + zb) % 2
    out_ref[0, slot] = flipped(whole([stream.f[...] for stream in home]))[:ops, :ops]
    for stream in home:
        stream.copy3.wait_recv()
    out_ref[0, 1 - slot] = whole([stream.r4[...] for stream in home])[:ops, :ops]

    to_side.wait_send()
    for copy in exchange:
        copy.wait_send()
    for stream in (*home, *near):
        for copy in (stream.copy0, stream.copy1, stream.copy2, stream.copy3):
            copy.wait_send()
    for stream in going:
        for copy in (stream.copy0, stream.copy1, *stream.home_copies):
            copy.wait_send()


def on_device(amplitudes):
    states, dets, ops = amplitudes.shape
    block = jnp.pad(amplitudes.transpose(0, 2, 1), ((0, 0), (0, -ops % 8), (0, 0)))
    dma = pltpu.SemaphoreType.DMA

    def tiles(*lead):
        return pltpu.VMEM((*lead, packed_rows(max(SIZES)), 128), jnp.float32)

    return pl.pallas_call(
        kernel,
        out_shape=jax.ShapeDtypeStruct((2, 2, ops, ops), jnp.float32),
        in_specs=[pl.BlockSpec(memory_space=pl.ANY)],
        out_specs=pl.BlockSpec(memory_space=pltpu.VMEM),
        scratch_shapes=[
            pltpu.VMEM((states, ROWS, dets), jnp.bfloat16),
            pltpu.VMEM((states, ROWS, dets), jnp.bfloat16),
            pltpu.VMEM((states, ROWS, dets // 2), jnp.bfloat16),
            tiles(STREAMS, 2, 2, 2),
            tiles(STREAMS, 2, 2),
            tiles(STREAMS, 2),
            tiles(STREAMS),
            tiles(STREAMS),
            tiles(STREAMS),
            tiles(CHUNKS, 2),
            dma((STREAMS * STEPS,)),
            dma((STREAMS * STEPS,)),
            dma,
            dma((CHUNKS + 1,)),
            dma((CHUNKS + 1,)),
        ],
        compiler_params=pltpu.CompilerParams(
            collective_id=0, has_side_effects=True, vmem_limit_bytes=64 * 1024 * 1024 - 65536,
        ),
    )(block)


def solution(mesh):
    fine = Mesh(mesh.devices.reshape(2, 2, 4, 2, 4, 2), ("zb", "za", "y", "core", "x", "zh"))
    state, det = ("zb", "za", "y", "core"), ("x", "zh")
    return jax.shard_map(
        on_device,
        mesh=fine,
        in_specs=(P(state, det, None),),
        out_specs=P(None, state + det, None, None),
        check_vma=False,
    )
```

```python
import jax
import jax.numpy as jnp
from jax import lax
from jax.experimental import pallas as pl
from jax.experimental.pallas import tpu as pltpu
from jax.sharding import Mesh, PartitionSpec as P

MESH = pl.DeviceIdType.MESH
ROWS = 336
LANES = 384
SIZES = (96, 96, 80, 64)
STARTS = (0, 96, 192, 272)
CHUNKS = len(SIZES)
HOME, AWAY, NEAR = 0, CHUNKS, 2 * CHUNKS
STREAMS = 3 * CHUNKS
STEPS = 4


def group_of(a, scheme):
    if scheme == 0:
        return ((a + 1) // 2) % 2, a // 2
    return a // 2, a % 2


def product(left, right):
    return lax.dot_general(left, right, (((1,), (1,)), ((), ())), preferred_element_type=jnp.float32)


def lanes(rows):
    return lax.broadcasted_iota(jnp.int32, (rows, 128), 1)


def packed_rows(size):
    return 2 * size + size // 2 + 8


def pack(tile):
    size, third = tile.shape[0], tile[:, 256:]
    if third.shape[1] < 128:
        third = jnp.concatenate([third, jnp.zeros((size, 128 - third.shape[1]), jnp.float32)], 1)
    folded = jnp.where(lanes(size // 2) < 64, third[:size // 2], pltpu.roll(third[size // 2:], 64, 1))
    rest = jnp.concatenate([third, jnp.zeros((128 - size, 128), jnp.float32)], 0).T[64:72]
    return jnp.concatenate([tile[:, :128], tile[:, 128:256], folded, rest], 0)


def unpack(packed, size):
    end = packed_rows(size)
    folded = packed[2 * size:end - 8]
    third = jnp.concatenate([folded, pltpu.roll(folded, 64, 1)], 0)
    rest = jnp.concatenate([packed[end - 8:], jnp.zeros((120, 128), jnp.float32)], 0).T[:size]
    third = jnp.where(lanes(size) < 64, third, pltpu.roll(rest, 64, 1))
    return jnp.concatenate([packed[:size], packed[size:2 * size], third], 1)


def whole(chunks):
    return jnp.concatenate([unpack(chunk, size) for chunk, size in zip(chunks, SIZES)], 0)


def flipped(tile):
    return jnp.concatenate([tile, jnp.zeros((LANES - ROWS, LANES), jnp.float32)], 0).T


def remote(source, target, sends, recvs, send_at, recv_at, device):
    return pltpu.make_async_remote_copy(
        src_ref=source, dst_ref=target, send_sem=sends.at[send_at], recv_sem=recvs.at[recv_at],
        device_id=device, device_id_type=MESH,
    )


def by_state(raw, first, target, c):
    start, size = STARTS[c], SIZES[c]

    @pl.loop(0, target.shape[2] // 256)
    def _(i):
        part = pl.ds(pl.multiple_of(i * 256, 256), 256)
        target[:, start:start + size, part] = jnp.swapaxes(raw[first:first + size, :, part], 0, 1)


class Stream:
    def __init__(self, index, scheme, refs, sems):
        rows = pl.ds(0, packed_rows(SIZES[index % CHUNKS]))
        t, r1, r2, r3, f, r4 = refs
        self.t, self.r1 = t.at[index, :, :, :, rows], r1.at[index, :, :, rows]
        self.r2 = r2.at[index, :, rows]
        self.r3, self.f, self.r4 = (ref.at[index, rows] for ref in (r3, f, r4))
        self.sems, self.sem = sems, STEPS * index
        x, self.zh = lax.axis_index("x"), lax.axis_index("zh")
        self.group, self.member = group_of(x, scheme)
        near, far = {"x": x + 1 - 2 * (x % 2)}, {"x": 3 - x}
        self.first, self.second = (near, far) if scheme == 0 else (far, near)

    def copy(self, step, source, target, device):
        return remote(source, target, *self.sems, self.sem + step, self.sem + step, device)

    def over_x(self):
        self.copy0 = self.copy(0, self.t.at[1 - self.group], self.r1, self.first)
        self.copy0.start()

    def over_x_again(self):
        self.copy0.wait_recv()
        g, m = self.group, self.member
        self.t[g, 1 - m] += self.r1[1 - m]
        self.copy1 = self.copy(1, self.t.at[g, 1 - m], self.r2, self.second)
        self.copy1.start()
        self.t[g, m] += self.r1[m]

    def over_zh(self):
        self.copy1.wait_recv()
        g, m, h = self.group, self.member, self.zh
        self.t[g, m, 1 - h] += self.r2[1 - h]
        self.copy2 = self.copy(2, self.t.at[g, m, 1 - h], self.r3, {"zh": 1 - h})
        self.copy2.start()
        self.t[g, m, h] += self.r2[h]

    def summed(self):
        self.copy2.wait_recv()
        return self.t[self.group, self.member, self.zh] + self.r3[...]

    def to_mirror(self, value, device):
        self.f[...] = value
        self.copy3 = self.copy(3, self.f, self.r4, device)
        self.copy3.start()

    def go_home(self, r5, homes):
        self.copy1.wait_recv()
        g, m = self.group, self.member
        for bh in range(2):
            self.t[g, m, bh] += self.r2[bh]
        self.home_copies = [
            remote(self.t.at[g, m, bh], r5.at[self.zh], *self.sems, self.sem + 2 + bh, self.sem + 2 + self.zh, homes[bh])
            for bh in range(2)
        ]
        for copy in self.home_copies:
            copy.start()
        return [
            remote(self.t.at[g, m, z], r5.at[z], *self.sems, self.sem + 2 + z, self.sem + 2 + z, homes[z])
            for z in range(2)
        ]


def kernel(
    a_ref, out_ref, own, beside, held, raw_own, raw_beside, raw_held, t, r1, r2, r3, f, r4, r5,
    send_sem, recv_sem, load_sem, ex_send, ex_recv,
):
    zb, core = lax.axis_index("zb"), lax.axis_index("core")
    x, zh = lax.axis_index("x"), lax.axis_index("zh")
    half = held.shape[2]
    ops = out_ref.shape[2]

    other = {"zb": 1 - zb}
    home_mirror = {**other, "x": 2 * zh + (x + zb) % 2, "zh": x // 2}
    from_mirror = {**other, "x": 2 * zh + (x + 1 - zb) % 2, "zh": x // 2}
    homes = [{**other, "zh": z} for z in range(2)]
    near_mirror = {"core": 1 - core, "x": 2 * zh + (x + core) % 2, "zh": x // 2}
    partners = [
        {"core": 1 - core}, {"x": x + 1 - 2 * (x % 2)}, {"x": 3 - x}, {"zh": 1 - zh},
        *homes, home_mirror, from_mirror, near_mirror,
    ]
    barrier = pltpu.get_barrier_semaphore()
    for partner in partners:
        pl.semaphore_signal(barrier, inc=1, device_id=partner, device_id_type=MESH)
    pl.semaphore_wait(barrier, len(partners))

    here = pl.ds(pl.multiple_of(zb * half, half), half)
    away = pl.ds(pl.multiple_of((1 - zb) * half, half), half)
    valid = [min(size, ops - start) for start, size in zip(STARTS, SIZES)]
    exchange = []
    for c in range(CHUNKS):
        rows = pl.ds(STARTS[c], valid[c])
        exchange.append(remote(a_ref.at[rows, :, away], raw_held.at[rows], ex_send, ex_recv, c, c, other))
    for copy in exchange[:-1]:
        copy.start()
    to_side = remote(
        a_ref, raw_beside.at[pl.ds(0, ops)], ex_send, ex_recv, CHUNKS, CHUNKS, {"core": 1 - core}
    )
    to_side.start()
    loads = [
        pltpu.make_async_copy(
            a_ref.at[pl.ds(STARTS[c], valid[c])], raw_own.at[c % 2, pl.ds(0, valid[c])], load_sem.at[c]
        )
        for c in range(CHUNKS)
    ]
    loads[0].start()
    for c in range(CHUNKS):
        if c + 1 < CHUNKS:
            loads[c + 1].start()
        loads[c].wait()
        by_state(raw_own.at[c % 2], 0, own, c)

    refs, sems = (t, r1, r2, r3, f, r4), (send_sem, recv_sem)
    home = [Stream(HOME + c, 0, refs, sems) for c in range(CHUNKS)]
    going = [Stream(AWAY + c, 1, refs, sems) for c in range(CHUNKS)]
    near = [Stream(NEAR + c, c % 2, refs, sems) for c in range(CHUNKS)]

    to_side.wait_recv()
    for c in range(CHUNKS):
        by_state(raw_beside, STARTS[c], beside, c)

    @pl.loop(0, 4)
    def _(a):
        for bh in range(2):
            tile = product(beside[2 * bh + (a + core) % 2], own[a])
            for c in range(CHUNKS):
                g, m = group_of(a, c % 2)
                near[c].t[g, m, bh] = pack(tile[STARTS[c]:STARTS[c] + SIZES[c]])

    for stream in near:
        stream.over_x()
    for stream in near:
        stream.over_x_again()

    arrivals = []

    def far_chunk(c):
        exchange[c].wait_recv()
        by_state(raw_held, STARTS[c], held, c)
        rows, size = pl.ds(STARTS[c], SIZES[c]), SIZES[c]

        @pl.loop(0, 4)
        def _(a):
            left = [held[2 * bh + (a + role + zb) % 2, rows, :] for role in range(2) for bh in range(2)]
            tile = product(jnp.concatenate(left, 0), own[a, :, here])
            g, m = group_of(a, 0)
            for bh in range(2):
                home[c].t[g, m, bh] = pack(tile[bh * size:(bh + 1) * size])
                going[c].t[bh, (a + 1 + zb) % 2, a // 2] = pack(tile[(2 + bh) * size:(3 + bh) * size])

        home[c].over_x()
        going[c].over_x()
        if c == 0:
            for stream in near:
                stream.over_zh()
            exchange[-1].start()
        home[c].over_x_again()
        going[c].over_x_again()
        home[c].over_zh()
        arrivals.append(going[c].go_home(r5.at[c, :, pl.ds(0, packed_rows(size))], homes))

    for c in range(CHUNKS):
        far_chunk(c)

    for stream in near:
        stream.to_mirror(stream.summed(), near_mirror)
    slot = (x + core) % 2
    out_ref[1, slot] = flipped(whole([stream.f[...] for stream in near]))[:ops, :ops]

    for c in range(CHUNKS):
        for copy in arrivals[c]:
            copy.wait_recv()
    ends = [packed_rows(size) for size in SIZES]
    helped = flipped(whole([r5[c, 0, :ends[c]] + r5[c, 1, :ends[c]] for c in range(CHUNKS)]))
    for c in range(CHUNKS):
        part = helped[STARTS[c]:STARTS[c] + SIZES[c]]
        home[c].to_mirror(home[c].summed() + pack(part), home_mirror)
    for stream in near:
        stream.copy3.wait_recv()
    out_ref[1, 1 - slot] = whole([stream.r4[...] for stream in near])[:ops, :ops]
    slot = (x + zb) % 2
    out_ref[0, slot] = flipped(whole([stream.f[...] for stream in home]))[:ops, :ops]
    for c in range(CHUNKS):
        home[c].copy3.wait_recv()
        rows = pl.ds(STARTS[c], valid[c])
        out_ref[0, 1 - slot, rows, :] = unpack(home[c].r4[...], SIZES[c])[:valid[c], :ops]

    to_side.wait_send()
    for copy in exchange:
        copy.wait_send()
    for stream in (*home, *near):
        for copy in (stream.copy0, stream.copy1, stream.copy2, stream.copy3):
            copy.wait_send()
    for stream in going:
        for copy in (stream.copy0, stream.copy1, *stream.home_copies):
            copy.wait_send()


def on_device(amplitudes):
    states, dets, ops = amplitudes.shape
    dma = pltpu.SemaphoreType.DMA

    def tiles(*lead):
        return pltpu.VMEM((*lead, packed_rows(max(SIZES)), 128), jnp.float32)

    return pl.pallas_call(
        kernel,
        out_shape=jax.ShapeDtypeStruct((2, 2, ops, ops), jnp.float32),
        in_specs=[pl.BlockSpec(memory_space=pl.ANY)],
        out_specs=pl.BlockSpec(memory_space=pltpu.VMEM),
        scratch_shapes=[
            pltpu.VMEM((states, ROWS, dets), jnp.bfloat16),
            pltpu.VMEM((states, ROWS, dets), jnp.bfloat16),
            pltpu.VMEM((states, ROWS, dets // 2), jnp.bfloat16),
            pltpu.VMEM((2, max(SIZES), states, dets), jnp.bfloat16),
            pltpu.VMEM((ROWS, states, dets), jnp.bfloat16),
            pltpu.VMEM((ROWS, states, dets // 2), jnp.bfloat16),
            tiles(STREAMS, 2, 2, 2),
            tiles(STREAMS, 2, 2),
            tiles(STREAMS, 2),
            tiles(STREAMS),
            tiles(STREAMS),
            tiles(STREAMS),
            tiles(CHUNKS, 2),
            dma((STREAMS * STEPS,)),
            dma((STREAMS * STEPS,)),
            dma((CHUNKS,)),
            dma((CHUNKS + 1,)),
            dma((CHUNKS + 1,)),
        ],
        compiler_params=pltpu.CompilerParams(
            collective_id=0, has_side_effects=True, vmem_limit_bytes=64 * 1024 * 1024 - 65536,
        ),
    )(amplitudes.transpose(2, 0, 1))


def solution(mesh):
    fine = Mesh(mesh.devices.reshape(2, 2, 4, 2, 4, 2), ("zb", "za", "y", "core", "x", "zh"))
    state, det = ("zb", "za", "y", "core"), ("x", "zh")
    return jax.shard_map(
        on_device,
        mesh=fine,
        in_specs=(P(state, det, None),),
        out_specs=P(None, state + det, None, None),
        check_vma=False,
    )
```

```python
import jax
import jax.numpy as jnp
from jax import lax
from jax.experimental import pallas as pl
from jax.experimental.pallas import tpu as pltpu
from jax.sharding import Mesh, PartitionSpec as P

MESH = pl.DeviceIdType.MESH
ROWS = 336
LANES = 384
SIZES = (96, 96, 80, 64)
STARTS = (0, 96, 192, 272)
CHUNKS = len(SIZES)
HOME, AWAY, NEAR = 0, CHUNKS, 2 * CHUNKS
STREAMS = 3 * CHUNKS
STEPS = 4


def group_of(a, scheme):
    if scheme == 0:
        return ((a + 1) // 2) % 2, a // 2
    return a // 2, a % 2


def product(left, right):
    return lax.dot_general(left, right, (((1,), (1,)), ((), ())), preferred_element_type=jnp.float32)


def lanes(rows):
    return lax.broadcasted_iota(jnp.int32, (rows, 128), 1)


def packed_rows(size):
    return 2 * size + size // 2 + 8


def pack(tile):
    size, third = tile.shape[0], tile[:, 256:]
    if third.shape[1] < 128:
        third = jnp.concatenate([third, jnp.zeros((size, 128 - third.shape[1]), jnp.float32)], 1)
    folded = jnp.where(lanes(size // 2) < 64, third[:size // 2], pltpu.roll(third[size // 2:], 64, 1))
    rest = jnp.concatenate([third, jnp.zeros((128 - size, 128), jnp.float32)], 0).T[64:72]
    return jnp.concatenate([tile[:, :128], tile[:, 128:256], folded, rest], 0)


def unpack(packed, size):
    end = packed_rows(size)
    folded = packed[2 * size:end - 8]
    third = jnp.concatenate([folded, pltpu.roll(folded, 64, 1)], 0)
    rest = jnp.concatenate([packed[end - 8:], jnp.zeros((120, 128), jnp.float32)], 0).T[:size]
    third = jnp.where(lanes(size) < 64, third, pltpu.roll(rest, 64, 1))
    return jnp.concatenate([packed[:size], packed[size:2 * size], third], 1)


def whole(chunks):
    return jnp.concatenate([unpack(chunk, size) for chunk, size in zip(chunks, SIZES)], 0)


def flipped(tile):
    return jnp.concatenate([tile, jnp.zeros((LANES - ROWS, LANES), jnp.float32)], 0).T


def remote(source, target, sends, recvs, send_at, recv_at, device):
    return pltpu.make_async_remote_copy(
        src_ref=source, dst_ref=target, send_sem=sends.at[send_at], recv_sem=recvs.at[recv_at],
        device_id=device, device_id_type=MESH,
    )


def by_state(raw, first, target, c):
    start, size = STARTS[c], SIZES[c]

    @pl.loop(0, target.shape[2] // 256)
    def _(i):
        part = pl.ds(pl.multiple_of(i * 256, 256), 256)
        target[:, start:start + size, part] = jnp.swapaxes(raw[first:first + size, :, part], 0, 1)


class Stream:
    def __init__(self, index, scheme, refs, sems):
        rows = pl.ds(0, packed_rows(SIZES[index % CHUNKS]))
        t, r1, r2, r3, f, r4 = refs
        self.t, self.r1 = t.at[index, :, :, :, rows], r1.at[index, :, :, rows]
        self.r2 = r2.at[index, :, rows]
        self.r3, self.f, self.r4 = (ref.at[index, rows] for ref in (r3, f, r4))
        self.sems, self.sem = sems, STEPS * index
        x, self.zh = lax.axis_index("x"), lax.axis_index("zh")
        self.group, self.member = group_of(x, scheme)
        near, far = {"x": x + 1 - 2 * (x % 2)}, {"x": 3 - x}
        self.first, self.second = (near, far) if scheme == 0 else (far, near)

    def copy(self, step, source, target, device):
        return remote(source, target, *self.sems, self.sem + step, self.sem + step, device)

    def over_x(self):
        self.copy0 = self.copy(0, self.t.at[1 - self.group], self.r1, self.first)
        self.copy0.start()

    def over_x_again(self):
        self.copy0.wait_recv()
        g, m = self.group, self.member
        self.t[g, 1 - m] += self.r1[1 - m]
        self.copy1 = self.copy(1, self.t.at[g, 1 - m], self.r2, self.second)
        self.copy1.start()
        self.t[g, m] += self.r1[m]

    def settle(self):
        self.copy1.wait_recv()
        for last in range(2):
            self.t[self.group, self.member, last] += self.r2[last]

    def add(self, last, value):
        self.t[self.group, self.member, last] += value

    def over_zh(self):
        self.copy2 = self.copy(2, self.t.at[self.group, self.member, 1 - self.zh], self.r3, {"zh": 1 - self.zh})
        self.copy2.start()

    def summed(self):
        self.copy2.wait_recv()
        return self.t[self.group, self.member, self.zh] + self.r3[...]

    def to_mirror(self, value, device):
        self.f[...] = value
        self.copy3 = self.copy(3, self.f, self.r4, device)
        self.copy3.start()

    def across(self, r5, device):
        self.copy2 = self.copy(2, self.t.at[self.group, self.member], r5, device)
        self.copy2.start()


def kernel(
    a_ref, out_ref, own, beside, held, raw_own, raw_beside, raw_held, t, r1, r2, r3, f, r4, r5,
    send_sem, recv_sem, load_sem, ex_send, ex_recv,
):
    zb, core = lax.axis_index("zb"), lax.axis_index("core")
    x, zh = lax.axis_index("x"), lax.axis_index("zh")
    half = held.shape[2]
    ops = out_ref.shape[2]

    other = {"zb": 1 - zb}
    home_mirror = {**other, "x": 2 * zh + (x + zb) % 2, "zh": x // 2}
    from_mirror = {**other, "x": 2 * zh + (x + 1 - zb) % 2, "zh": x // 2}
    joint = {**other, "zh": 1 - zh}
    near_mirror = {"core": 1 - core, "x": 2 * zh + (x + core) % 2, "zh": x // 2}
    partners = [
        {"core": 1 - core}, {"x": x + 1 - 2 * (x % 2)}, {"x": 3 - x}, {"zh": 1 - zh},
        other, joint, home_mirror, from_mirror, near_mirror,
    ]
    barrier = pltpu.get_barrier_semaphore()
    for partner in partners:
        pl.semaphore_signal(barrier, inc=1, device_id=partner, device_id_type=MESH)
    pl.semaphore_wait(barrier, len(partners))

    here = pl.ds(pl.multiple_of(zb * half, half), half)
    away = pl.ds(pl.multiple_of((1 - zb) * half, half), half)
    valid = [min(size, ops - start) for start, size in zip(STARTS, SIZES)]
    exchange = []
    for c in range(CHUNKS):
        rows = pl.ds(STARTS[c], valid[c])
        exchange.append(remote(a_ref.at[rows, :, away], raw_held.at[rows], ex_send, ex_recv, c, c, other))
    for copy in exchange:
        copy.start()
    to_side = remote(
        a_ref, raw_beside.at[pl.ds(0, ops)], ex_send, ex_recv, CHUNKS, CHUNKS, {"core": 1 - core}
    )
    to_side.start()
    loads = [
        pltpu.make_async_copy(
            a_ref.at[pl.ds(STARTS[c], valid[c])], raw_own.at[c % 2, pl.ds(0, valid[c])], load_sem.at[c]
        )
        for c in range(CHUNKS)
    ]
    loads[0].start()
    for c in range(CHUNKS):
        if c + 1 < CHUNKS:
            loads[c + 1].start()
        loads[c].wait()
        by_state(raw_own.at[c % 2], 0, own, c)

    refs, sems = (t, r1, r2, r3, f, r4), (send_sem, recv_sem)
    home = [Stream(HOME + c, 0, refs, sems) for c in range(CHUNKS)]
    going = [Stream(AWAY + c, 1, refs, sems) for c in range(CHUNKS)]
    near = [Stream(NEAR + c, c % 2, refs, sems) for c in range(CHUNKS)]

    to_side.wait_recv()
    for c in range(CHUNKS):
        by_state(raw_beside, STARTS[c], beside, c)

    @pl.loop(0, 4)
    def _(a):
        for bh in range(2):
            tile = product(beside[2 * bh + (a + core) % 2], own[a])
            for c in range(CHUNKS):
                g, m = group_of(a, c % 2)
                near[c].t[g, m, bh] = pack(tile[STARTS[c]:STARTS[c] + SIZES[c]])

    for stream in near:
        stream.over_x()
    for stream in near:
        stream.over_x_again()

    def far_chunk(c):
        exchange[c].wait_recv()
        by_state(raw_held, STARTS[c], held, c)
        rows, size = pl.ds(STARTS[c], SIZES[c]), SIZES[c]

        @pl.loop(0, 4)
        def _(a):
            left = [held[2 * bh + (a + role + zb) % 2, rows, :] for role in range(2) for bh in range(2)]
            tile = product(jnp.concatenate(left, 0), own[a, :, here])
            g, m = group_of(a, 0)
            for bh in range(2):
                home[c].t[g, m, bh] = pack(tile[bh * size:(bh + 1) * size])
                going[c].t[bh, (a + 1 + zb) % 2, a // 2] = pack(tile[(2 + bh) * size:(3 + bh) * size])

        home[c].over_x()
        going[c].over_x()
        if c == 0:
            for stream in near:
                stream.settle()
                stream.over_zh()
        home[c].over_x_again()
        going[c].over_x_again()
        going[c].settle()
        going[c].across(r5.at[c, :, pl.ds(0, packed_rows(size))], joint)
        home[c].settle()

    for c in range(CHUNKS):
        far_chunk(c)

    for stream in near:
        stream.to_mirror(stream.summed(), near_mirror)
    slot = (x + core) % 2
    out_ref[1, slot] = flipped(whole([stream.f[...] for stream in near]))[:ops, :ops]

    for stream in going:
        stream.copy2.wait_recv()
    for last in (1 - zh, zh):
        helped = flipped(whole([r5[c, last, :packed_rows(SIZES[c])] for c in range(CHUNKS)]))
        for c in range(CHUNKS):
            home[c].add(last, pack(helped[STARTS[c]:STARTS[c] + SIZES[c]]))
        if last is not zh:
            for stream in home:
                stream.over_zh()
    for stream in home:
        stream.to_mirror(stream.summed(), home_mirror)
    for stream in near:
        stream.copy3.wait_recv()
    out_ref[1, 1 - slot] = whole([stream.r4[...] for stream in near])[:ops, :ops]
    slot = (x + zb) % 2
    out_ref[0, slot] = flipped(whole([stream.f[...] for stream in home]))[:ops, :ops]
    for c in range(CHUNKS):
        home[c].copy3.wait_recv()
        rows = pl.ds(STARTS[c], valid[c])
        out_ref[0, 1 - slot, rows, :] = unpack(home[c].r4[...], SIZES[c])[:valid[c], :ops]

    to_side.wait_send()
    for copy in exchange:
        copy.wait_send()
    for stream in (*home, *going, *near):
        for copy in (stream.copy0, stream.copy1, stream.copy2):
            copy.wait_send()
    for stream in (*home, *near):
        stream.copy3.wait_send()


def on_device(amplitudes):
    states, dets, ops = amplitudes.shape
    dma = pltpu.SemaphoreType.DMA

    def tiles(*lead):
        return pltpu.VMEM((*lead, packed_rows(max(SIZES)), 128), jnp.float32)

    return pl.pallas_call(
        kernel,
        out_shape=jax.ShapeDtypeStruct((2, 2, ops, ops), jnp.float32),
        in_specs=[pl.BlockSpec(memory_space=pl.ANY)],
        out_specs=pl.BlockSpec(memory_space=pltpu.VMEM),
        scratch_shapes=[
            pltpu.VMEM((states, ROWS, dets), jnp.bfloat16),
            pltpu.VMEM((states, ROWS, dets), jnp.bfloat16),
            pltpu.VMEM((states, ROWS, dets // 2), jnp.bfloat16),
            pltpu.VMEM((2, max(SIZES), states, dets), jnp.bfloat16),
            pltpu.VMEM((ROWS, states, dets), jnp.bfloat16),
            pltpu.VMEM((ROWS, states, dets // 2), jnp.bfloat16),
            tiles(STREAMS, 2, 2, 2),
            tiles(STREAMS, 2, 2),
            tiles(STREAMS, 2),
            tiles(STREAMS),
            tiles(STREAMS),
            tiles(STREAMS),
            tiles(CHUNKS, 2),
            dma((STREAMS * STEPS,)),
            dma((STREAMS * STEPS,)),
            dma((CHUNKS,)),
            dma((CHUNKS + 1,)),
            dma((CHUNKS + 1,)),
        ],
        compiler_params=pltpu.CompilerParams(
            collective_id=0, has_side_effects=True, vmem_limit_bytes=64 * 1024 * 1024 - 65536,
        ),
    )(amplitudes.transpose(2, 0, 1))


def solution(mesh):
    fine = Mesh(mesh.devices.reshape(2, 2, 4, 2, 4, 2), ("zb", "za", "y", "core", "x", "zh"))
    state, det = ("zb", "za", "y", "core"), ("x", "zh")
    return jax.shard_map(
        on_device,
        mesh=fine,
        in_specs=(P(state, det, None),),
        out_specs=P(None, state + det, None, None),
        check_vma=False,
    )
```

```python
import jax
import jax.numpy as jnp
from jax import lax
from jax.experimental import pallas as pl
from jax.experimental.pallas import tpu as pltpu
from jax.sharding import Mesh, PartitionSpec as P

MESH = pl.DeviceIdType.MESH
ROWS = 336
LANES = 384
SIZES = (96, 96, 80, 64)
STARTS = (0, 96, 192, 272)
CHUNKS = len(SIZES)
HOME, AWAY, NEAR = 0, CHUNKS, 2 * CHUNKS
STREAMS = 3 * CHUNKS
STEPS = 4


def group_of(a, scheme):
    if scheme == 0:
        return ((a + 1) // 2) % 2, a // 2
    return a // 2, a % 2


def product(left, right):
    return lax.dot_general(left, right, (((1,), (1,)), ((), ())), preferred_element_type=jnp.float32)


def lanes(rows):
    return lax.broadcasted_iota(jnp.int32, (rows, 128), 1)


def packed_rows(size):
    return 2 * size + size // 2 + 8


def pack(tile):
    size, third = tile.shape[0], tile[:, 256:]
    if third.shape[1] < 128:
        third = jnp.concatenate([third, jnp.zeros((size, 128 - third.shape[1]), jnp.float32)], 1)
    folded = jnp.where(lanes(size // 2) < 64, third[:size // 2], pltpu.roll(third[size // 2:], 64, 1))
    rest = jnp.concatenate([third, jnp.zeros((128 - size, 128), jnp.float32)], 0).T[64:72]
    return jnp.concatenate([tile[:, :128], tile[:, 128:256], folded, rest], 0)


def unpack(packed, size):
    end = packed_rows(size)
    folded = packed[2 * size:end - 8]
    third = jnp.concatenate([folded, pltpu.roll(folded, 64, 1)], 0)
    rest = jnp.concatenate([packed[end - 8:], jnp.zeros((120, 128), jnp.float32)], 0).T[:size]
    third = jnp.where(lanes(size) < 64, third, pltpu.roll(rest, 64, 1))
    return jnp.concatenate([packed[:size], packed[size:2 * size], third], 1)


def whole(chunks):
    return jnp.concatenate([unpack(chunk, size) for chunk, size in zip(chunks, SIZES)], 0)


def flipped(tile):
    return jnp.concatenate([tile, jnp.zeros((LANES - ROWS, LANES), jnp.float32)], 0).T


def remote(source, target, sends, recvs, send_at, recv_at, device):
    return pltpu.make_async_remote_copy(
        src_ref=source, dst_ref=target, send_sem=sends.at[send_at], recv_sem=recvs.at[recv_at],
        device_id=device, device_id_type=MESH,
    )


def by_state(raw, first, target, c):
    start, size = STARTS[c], SIZES[c]

    @pl.loop(0, target.shape[2] // 256)
    def _(i):
        part = pl.ds(pl.multiple_of(i * 256, 256), 256)
        target[:, start:start + size, part] = jnp.swapaxes(raw[first:first + size, :, part], 0, 1)


class Stream:
    def __init__(self, index, scheme, refs, sems):
        rows = pl.ds(0, packed_rows(SIZES[index % CHUNKS]))
        t, r1, r2, r3, f, r4 = refs
        self.t, self.r1 = t.at[index, :, :, :, rows], r1.at[index, :, :, rows]
        self.r2 = r2.at[index, :, rows]
        self.r3, self.f, self.r4 = (ref.at[index, rows] for ref in (r3, f, r4))
        self.sems, self.sem = sems, STEPS * index
        x, self.zh = lax.axis_index("x"), lax.axis_index("zh")
        self.group, self.member = group_of(x, scheme)
        near, far = {"x": x + 1 - 2 * (x % 2)}, {"x": 3 - x}
        self.first, self.second = (near, far) if scheme == 0 else (far, near)

    def copy(self, step, source, target, device):
        return remote(source, target, *self.sems, self.sem + step, self.sem + step, device)

    def over_x(self):
        self.copy0 = self.copy(0, self.t.at[1 - self.group], self.r1, self.first)
        self.copy0.start()

    def over_x_again(self):
        self.copy0.wait_recv()
        g, m = self.group, self.member
        self.t[g, 1 - m] += self.r1[1 - m]
        self.copy1 = self.copy(1, self.t.at[g, 1 - m], self.r2, self.second)
        self.copy1.start()
        self.t[g, m] += self.r1[m]

    def settle(self):
        self.copy1.wait_recv()
        for last in range(2):
            self.t[self.group, self.member, last] += self.r2[last]

    def add(self, last, value):
        self.t[self.group, self.member, last] += value

    def over_zh(self):
        self.copy2 = self.copy(2, self.t.at[self.group, self.member, 1 - self.zh], self.r3, {"zh": 1 - self.zh})
        self.copy2.start()

    def summed(self):
        self.copy2.wait_recv()
        return self.t[self.group, self.member, self.zh] + self.r3[...]

    def to_mirror(self, value, device):
        self.f[...] = value
        self.copy3 = self.copy(3, self.f, self.r4, device)
        self.copy3.start()

    def across(self, r5, device):
        self.copy2 = self.copy(2, self.t.at[self.group, self.member], r5, device)
        self.copy2.start()


def kernel(
    a_ref, out_ref, own, beside, held, raw_own, raw_beside, raw_held, t, r1, r2, r3, f, r4, r5,
    send_sem, recv_sem, load_sem, ex_send, ex_recv,
):
    zb, core = lax.axis_index("zb"), lax.axis_index("core")
    x, zh = lax.axis_index("x"), lax.axis_index("zh")
    half = held.shape[2]
    ops = out_ref.shape[2]

    other = {"zb": 1 - zb}
    home_mirror = {**other, "x": 2 * zh + (x + zb) % 2, "zh": x // 2}
    from_mirror = {**other, "x": 2 * zh + (x + 1 - zb) % 2, "zh": x // 2}
    joint = {**other, "zh": 1 - zh}
    near_mirror = {"core": 1 - core, "x": 2 * zh + (x + core) % 2, "zh": x // 2}
    partners = [
        {"core": 1 - core}, {"x": x + 1 - 2 * (x % 2)}, {"x": 3 - x}, {"zh": 1 - zh},
        other, joint, home_mirror, from_mirror, near_mirror,
    ]
    barrier = pltpu.get_barrier_semaphore()
    for partner in partners:
        pl.semaphore_signal(barrier, inc=1, device_id=partner, device_id_type=MESH)
    pl.semaphore_wait(barrier, len(partners))

    here = pl.ds(pl.multiple_of(zb * half, half), half)
    away = pl.ds(pl.multiple_of((1 - zb) * half, half), half)
    valid = [min(size, ops - start) for start, size in zip(STARTS, SIZES)]
    exchange = []
    for c in range(CHUNKS):
        rows = pl.ds(STARTS[c], valid[c])
        exchange.append(remote(a_ref.at[rows, :, away], raw_held.at[rows], ex_send, ex_recv, c, c, other))
    for copy in exchange:
        copy.start()
    to_side = remote(
        a_ref, raw_beside.at[pl.ds(0, ops)], ex_send, ex_recv, CHUNKS, CHUNKS, {"core": 1 - core}
    )
    to_side.start()
    loads = [
        pltpu.make_async_copy(
            a_ref.at[pl.ds(STARTS[c], valid[c])], raw_own.at[c % 2, pl.ds(0, valid[c])], load_sem.at[c]
        )
        for c in range(CHUNKS)
    ]
    loads[0].start()
    for c in range(CHUNKS):
        if c + 1 < CHUNKS:
            loads[c + 1].start()
        loads[c].wait()
        by_state(raw_own.at[c % 2], 0, own, c)

    refs, sems = (t, r1, r2, r3, f, r4), (send_sem, recv_sem)
    home = [Stream(HOME + c, 0, refs, sems) for c in range(CHUNKS)]
    going = [Stream(AWAY + c, 1, refs, sems) for c in range(CHUNKS)]
    near = [Stream(NEAR + c, c % 2, refs, sems) for c in range(CHUNKS)]

    to_side.wait_recv()
    for c in range(CHUNKS):
        by_state(raw_beside, STARTS[c], beside, c)

    @pl.loop(0, 4)
    def _(a):
        for bh in range(2):
            tile = product(beside[2 * bh + (a + core) % 2], own[a])
            for c in range(CHUNKS):
                g, m = group_of(a, c % 2)
                near[c].t[g, m, bh] = pack(tile[STARTS[c]:STARTS[c] + SIZES[c]])

    for stream in near:
        stream.over_x()
    for stream in near:
        stream.over_x_again()

    def far_chunk(c):
        exchange[c].wait_recv()
        by_state(raw_held, STARTS[c], held, c)
        rows, size = pl.ds(STARTS[c], SIZES[c]), SIZES[c]

        @pl.loop(0, 4)
        def _(a):
            left = [held[2 * bh + (a + role + zb) % 2, rows, :] for role in range(2) for bh in range(2)]
            tile = product(jnp.concatenate(left, 0), own[a, :, here])
            g, m = group_of(a, 0)
            for bh in range(2):
                home[c].t[g, m, bh] = pack(tile[bh * size:(bh + 1) * size])
                going[c].t[bh, (a + 1 + zb) % 2, a // 2] = pack(tile[(2 + bh) * size:(3 + bh) * size])

        home[c].over_x()
        going[c].over_x()

    def again(c):
        home[c].over_x_again()
        going[c].over_x_again()

    def join(c):
        going[c].settle()
        going[c].across(r5.at[c, :, pl.ds(0, packed_rows(SIZES[c]))], joint)
        home[c].settle()

    for c in range(CHUNKS):
        far_chunk(c)
        if c == 0:
            for stream in near:
                stream.settle()
                stream.over_zh()
        if c >= 1:
            again(c - 1)
        if c >= 2:
            join(c - 2)

    for stream in near:
        stream.to_mirror(stream.summed(), near_mirror)
    again(CHUNKS - 1)
    join(CHUNKS - 2)
    join(CHUNKS - 1)

    for stream in going:
        stream.copy2.wait_recv()
    for last in (1 - zh, zh):
        helped = flipped(whole([r5[c, last, :packed_rows(SIZES[c])] for c in range(CHUNKS)]))
        for c in range(CHUNKS):
            home[c].add(last, pack(helped[STARTS[c]:STARTS[c] + SIZES[c]]))
        if last is not zh:
            for stream in home:
                stream.over_zh()
    slot = (x + core) % 2
    out_ref[1, slot] = flipped(whole([stream.f[...] for stream in near]))[:ops, :ops]
    for stream in home:
        stream.to_mirror(stream.summed(), home_mirror)
    for stream in near:
        stream.copy3.wait_recv()
    out_ref[1, 1 - slot] = whole([stream.r4[...] for stream in near])[:ops, :ops]
    slot = (x + zb) % 2
    out_ref[0, slot] = flipped(whole([stream.f[...] for stream in home]))[:ops, :ops]
    for c in range(CHUNKS):
        home[c].copy3.wait_recv()
        rows = pl.ds(STARTS[c], valid[c])
        out_ref[0, 1 - slot, rows, :] = unpack(home[c].r4[...], SIZES[c])[:valid[c], :ops]

    to_side.wait_send()
    for copy in exchange:
        copy.wait_send()
    for stream in (*home, *going, *near):
        for copy in (stream.copy0, stream.copy1, stream.copy2):
            copy.wait_send()
    for stream in (*home, *near):
        stream.copy3.wait_send()


def on_device(amplitudes):
    states, dets, ops = amplitudes.shape
    dma = pltpu.SemaphoreType.DMA

    def tiles(*lead):
        return pltpu.VMEM((*lead, packed_rows(max(SIZES)), 128), jnp.float32)

    return pl.pallas_call(
        kernel,
        out_shape=jax.ShapeDtypeStruct((2, 2, ops, ops), jnp.float32),
        in_specs=[pl.BlockSpec(memory_space=pl.ANY)],
        out_specs=pl.BlockSpec(memory_space=pltpu.VMEM),
        scratch_shapes=[
            pltpu.VMEM((states, ROWS, dets), jnp.bfloat16),
            pltpu.VMEM((states, ROWS, dets), jnp.bfloat16),
            pltpu.VMEM((states, ROWS, dets // 2), jnp.bfloat16),
            pltpu.VMEM((2, max(SIZES), states, dets), jnp.bfloat16),
            pltpu.VMEM((ROWS, states, dets), jnp.bfloat16),
            pltpu.VMEM((ROWS, states, dets // 2), jnp.bfloat16),
            tiles(STREAMS, 2, 2, 2),
            tiles(STREAMS, 2, 2),
            tiles(STREAMS, 2),
            tiles(STREAMS),
            tiles(STREAMS),
            tiles(STREAMS),
            tiles(CHUNKS, 2),
            dma((STREAMS * STEPS,)),
            dma((STREAMS * STEPS,)),
            dma((CHUNKS,)),
            dma((CHUNKS + 1,)),
            dma((CHUNKS + 1,)),
        ],
        compiler_params=pltpu.CompilerParams(
            collective_id=0, has_side_effects=True, vmem_limit_bytes=64 * 1024 * 1024 - 65536,
        ),
    )(amplitudes.transpose(2, 0, 1))


def solution(mesh):
    fine = Mesh(mesh.devices.reshape(2, 2, 4, 2, 4, 2), ("zb", "za", "y", "core", "x", "zh"))
    state, det = ("zb", "za", "y", "core"), ("x", "zh")
    return jax.shard_map(
        on_device,
        mesh=fine,
        in_specs=(P(state, det, None),),
        out_specs=P(None, state + det, None, None),
        check_vma=False,
    )
```

```python
import jax
import jax.numpy as jnp
from jax import lax
from jax.experimental import pallas as pl
from jax.experimental.pallas import tpu as pltpu
from jax.sharding import Mesh, PartitionSpec as P

MESH = pl.DeviceIdType.MESH
ROWS = 336
LANES = 384
SIZES = (96, 96, 80, 64)
STARTS = (0, 96, 192, 272)
CHUNKS = len(SIZES)
HOME, AWAY, NEAR = 0, CHUNKS, 2 * CHUNKS
STREAMS = 3 * CHUNKS
STEPS = 4


def group_of(a, scheme):
    if scheme == 0:
        return ((a + 1) // 2) % 2, a // 2
    return a // 2, a % 2


def product(left, right):
    return lax.dot_general(left, right, (((1,), (1,)), ((), ())), preferred_element_type=jnp.float32)


def lanes(rows):
    return lax.broadcasted_iota(jnp.int32, (rows, 128), 1)


def packed_rows(size):
    return 2 * size + size // 2 + 8


def pack(tile):
    size, third = tile.shape[0], tile[:, 256:]
    if third.shape[1] < 128:
        third = jnp.concatenate([third, jnp.zeros((size, 128 - third.shape[1]), jnp.float32)], 1)
    folded = jnp.where(lanes(size // 2) < 64, third[:size // 2], pltpu.roll(third[size // 2:], 64, 1))
    rest = jnp.concatenate([third, jnp.zeros((128 - size, 128), jnp.float32)], 0).T[64:72]
    return jnp.concatenate([tile[:, :128], tile[:, 128:256], folded, rest], 0)


def unpack(packed, size):
    end = packed_rows(size)
    folded = packed[2 * size:end - 8]
    third = jnp.concatenate([folded, pltpu.roll(folded, 64, 1)], 0)
    rest = jnp.concatenate([packed[end - 8:], jnp.zeros((120, 128), jnp.float32)], 0).T[:size]
    third = jnp.where(lanes(size) < 64, third, pltpu.roll(rest, 64, 1))
    return jnp.concatenate([packed[:size], packed[size:2 * size], third], 1)


def whole(chunks):
    return jnp.concatenate([unpack(chunk, size) for chunk, size in zip(chunks, SIZES)], 0)


def flipped(tile):
    return jnp.concatenate([tile, jnp.zeros((LANES - ROWS, LANES), jnp.float32)], 0).T


def remote(source, target, sends, recvs, send_at, recv_at, device):
    return pltpu.make_async_remote_copy(
        src_ref=source, dst_ref=target, send_sem=sends.at[send_at], recv_sem=recvs.at[recv_at],
        device_id=device, device_id_type=MESH,
    )


def by_state(raw, first, target, c):
    start, size = STARTS[c], SIZES[c]

    @pl.loop(0, target.shape[2] // 256)
    def _(i):
        part = pl.ds(pl.multiple_of(i * 256, 256), 256)
        target[:, start:start + size, part] = jnp.swapaxes(raw[first:first + size, :, part], 0, 1)


class Stream:
    def __init__(self, index, scheme, refs, sems):
        rows = pl.ds(0, packed_rows(SIZES[index % CHUNKS]))
        t, r1, r2, r3, f, r4 = refs
        self.t, self.r1 = t.at[index, :, :, :, rows], r1.at[index, :, :, rows]
        self.r2 = r2.at[index, :, rows]
        self.r3, self.f, self.r4 = (ref.at[index, rows] for ref in (r3, f, r4))
        self.sems, self.sem = sems, STEPS * index
        x, self.zh = lax.axis_index("x"), lax.axis_index("zh")
        self.group, self.member = group_of(x, scheme)
        near, far = {"x": x + 1 - 2 * (x % 2)}, {"x": 3 - x}
        self.first, self.second = (near, far) if scheme == 0 else (far, near)

    def copy(self, step, source, target, device):
        return remote(source, target, *self.sems, self.sem + step, self.sem + step, device)

    def over_x(self):
        self.copy0 = self.copy(0, self.t.at[1 - self.group], self.r1, self.first)
        self.copy0.start()

    def over_x_again(self):
        self.copy0.wait_recv()
        g, m = self.group, self.member
        self.t[g, 1 - m] += self.r1[1 - m]
        self.copy1 = self.copy(1, self.t.at[g, 1 - m], self.r2, self.second)
        self.copy1.start()
        self.t[g, m] += self.r1[m]

    def settle(self):
        self.copy1.wait_recv()
        for last in range(2):
            self.t[self.group, self.member, last] += self.r2[last]

    def add(self, last, value):
        self.t[self.group, self.member, last] += value

    def over_zh(self):
        self.copy2 = self.copy(2, self.t.at[self.group, self.member, 1 - self.zh], self.r3, {"zh": 1 - self.zh})
        self.copy2.start()

    def summed(self):
        self.copy2.wait_recv()
        return self.t[self.group, self.member, self.zh] + self.r3[...]

    def to_mirror(self, value, device):
        self.f[...] = value
        self.copy3 = self.copy(3, self.f, self.r4, device)
        self.copy3.start()

    def across(self, r5, device):
        self.copy2 = self.copy(2, self.t.at[self.group, self.member], r5, device)
        self.copy2.start()


def kernel(
    a_ref, out_ref, own, beside, held, raw_own, raw_beside, raw_held, t, r1, r2, r3, f, r4, r5,
    send_sem, recv_sem, load_sem, ex_send, ex_recv, credit,
):
    za, zb, core = lax.axis_index("za"), lax.axis_index("zb"), lax.axis_index("core")
    x, zh = lax.axis_index("x"), lax.axis_index("zh")
    half = held.shape[2]
    ops = out_ref.shape[2]

    other = {"zb": 1 - zb}
    home_mirror = {**other, "x": 2 * zh + (x + zb) % 2, "zh": x // 2}
    from_mirror = {**other, "x": 2 * zh + (x + 1 - zb) % 2, "zh": x // 2}
    joint = {**other, "zh": 1 - zh}
    beyond = {"za": 1 - za, "zb": 1 - zb}
    near_mirror = {"core": 1 - core, "x": 2 * zh + (x + core) % 2, "zh": x // 2}
    partners = [
        {"core": 1 - core}, {"x": x + 1 - 2 * (x % 2)}, {"x": 3 - x}, {"zh": 1 - zh},
        other, joint, beyond, home_mirror, from_mirror, near_mirror,
    ]
    barrier = pltpu.get_barrier_semaphore()
    for partner in partners:
        pl.semaphore_signal(barrier, inc=1, device_id=partner, device_id_type=MESH)
    pl.semaphore_wait(barrier, len(partners))

    here = pl.ds(pl.multiple_of(zb * half, half), half)
    away = pl.ds(pl.multiple_of((1 - zb) * half, half), half)
    valid = [min(size, ops - start) for start, size in zip(STARTS, SIZES)]
    exchange = []
    for c in range(CHUNKS):
        rows = pl.ds(STARTS[c], valid[c])
        exchange.append(remote(a_ref.at[rows, :, away], raw_held.at[rows], ex_send, ex_recv, c, c, other))
    exchange[0].start()

    @pl.when(za == zb)
    def _():
        for copy in exchange[1:]:
            copy.start()

    def arrive(c):
        exchange[c].wait_recv()
        if c + 1 < CHUNKS:

            @pl.when(za != zb)
            def _():
                pl.semaphore_signal(credit, inc=1, device_id=beyond, device_id_type=MESH)
                pl.semaphore_wait(credit, 1)
                exchange[c + 1].start()

    to_side = remote(
        a_ref, raw_beside.at[pl.ds(0, ops)], ex_send, ex_recv, CHUNKS, CHUNKS, {"core": 1 - core}
    )
    to_side.start()
    loads = [
        pltpu.make_async_copy(
            a_ref.at[pl.ds(STARTS[c], valid[c])], raw_own.at[c % 2, pl.ds(0, valid[c])], load_sem.at[c]
        )
        for c in range(CHUNKS)
    ]
    loads[0].start()
    for c in range(CHUNKS):
        if c + 1 < CHUNKS:
            loads[c + 1].start()
        loads[c].wait()
        by_state(raw_own.at[c % 2], 0, own, c)

    refs, sems = (t, r1, r2, r3, f, r4), (send_sem, recv_sem)
    home = [Stream(HOME + c, 0, refs, sems) for c in range(CHUNKS)]
    going = [Stream(AWAY + c, 1, refs, sems) for c in range(CHUNKS)]
    near = [Stream(NEAR + c, c % 2, refs, sems) for c in range(CHUNKS)]

    to_side.wait_recv()
    for c in range(CHUNKS):
        by_state(raw_beside, STARTS[c], beside, c)

    @pl.loop(0, 4)
    def _(a):
        for bh in range(2):
            tile = product(beside[2 * bh + (a + core) % 2], own[a])
            for c in range(CHUNKS):
                g, m = group_of(a, c % 2)
                near[c].t[g, m, bh] = pack(tile[STARTS[c]:STARTS[c] + SIZES[c]])

    for stream in near:
        stream.over_x()
    arrive(0)
    for stream in near:
        stream.over_x_again()

    def far_chunk(c):
        if c > 0:
            arrive(c)
        by_state(raw_held, STARTS[c], held, c)
        rows, size = pl.ds(STARTS[c], SIZES[c]), SIZES[c]

        @pl.loop(0, 4)
        def _(a):
            left = [held[2 * bh + (a + role + zb) % 2, rows, :] for role in range(2) for bh in range(2)]
            tile = product(jnp.concatenate(left, 0), own[a, :, here])
            g, m = group_of(a, 0)
            for bh in range(2):
                home[c].t[g, m, bh] = pack(tile[bh * size:(bh + 1) * size])
                going[c].t[bh, (a + 1 + zb) % 2, a // 2] = pack(tile[(2 + bh) * size:(3 + bh) * size])

        home[c].over_x()
        going[c].over_x()

    def again(c):
        home[c].over_x_again()
        going[c].over_x_again()

    def join(c):
        going[c].settle()
        going[c].across(r5.at[c, :, pl.ds(0, packed_rows(SIZES[c]))], joint)
        home[c].settle()

    for c in range(CHUNKS):
        far_chunk(c)
        if c + 1 == CHUNKS:
            for stream in near:
                stream.settle()
                stream.over_zh()
        if c >= 1:
            again(c - 1)
        if c >= 2:
            join(c - 2)

    again(CHUNKS - 1)
    join(CHUNKS - 2)
    join(CHUNKS - 1)
    for stream in near:
        stream.to_mirror(stream.summed(), near_mirror)

    for stream in going:
        stream.copy2.wait_recv()
    for last in (1 - zh, zh):
        helped = flipped(whole([r5[c, last, :packed_rows(SIZES[c])] for c in range(CHUNKS)]))
        for c in range(CHUNKS):
            home[c].add(last, pack(helped[STARTS[c]:STARTS[c] + SIZES[c]]))
        if last is not zh:
            for stream in home:
                stream.over_zh()
    slot = (x + core) % 2
    out_ref[1, slot] = flipped(whole([stream.f[...] for stream in near]))[:ops, :ops]
    for stream in home:
        stream.to_mirror(stream.summed(), home_mirror)
    for stream in near:
        stream.copy3.wait_recv()
    out_ref[1, 1 - slot] = whole([stream.r4[...] for stream in near])[:ops, :ops]
    slot = (x + zb) % 2
    out_ref[0, slot] = flipped(whole([stream.f[...] for stream in home]))[:ops, :ops]
    for c in range(CHUNKS):
        home[c].copy3.wait_recv()
        rows = pl.ds(STARTS[c], valid[c])
        out_ref[0, 1 - slot, rows, :] = unpack(home[c].r4[...], SIZES[c])[:valid[c], :ops]

    to_side.wait_send()
    for copy in exchange:
        copy.wait_send()
    for stream in (*home, *going, *near):
        for copy in (stream.copy0, stream.copy1, stream.copy2):
            copy.wait_send()
    for stream in (*home, *near):
        stream.copy3.wait_send()


def on_device(amplitudes):
    states, dets, ops = amplitudes.shape
    dma = pltpu.SemaphoreType.DMA

    def tiles(*lead):
        return pltpu.VMEM((*lead, packed_rows(max(SIZES)), 128), jnp.float32)

    return pl.pallas_call(
        kernel,
        out_shape=jax.ShapeDtypeStruct((2, 2, ops, ops), jnp.float32),
        in_specs=[pl.BlockSpec(memory_space=pl.ANY)],
        out_specs=pl.BlockSpec(memory_space=pltpu.VMEM),
        scratch_shapes=[
            pltpu.VMEM((states, ROWS, dets), jnp.bfloat16),
            pltpu.VMEM((states, ROWS, dets), jnp.bfloat16),
            pltpu.VMEM((states, ROWS, dets // 2), jnp.bfloat16),
            pltpu.VMEM((2, max(SIZES), states, dets), jnp.bfloat16),
            pltpu.VMEM((ROWS, states, dets), jnp.bfloat16),
            pltpu.VMEM((ROWS, states, dets // 2), jnp.bfloat16),
            tiles(STREAMS, 2, 2, 2),
            tiles(STREAMS, 2, 2),
            tiles(STREAMS, 2),
            tiles(STREAMS),
            tiles(STREAMS),
            tiles(STREAMS),
            tiles(CHUNKS, 2),
            dma((STREAMS * STEPS,)),
            dma((STREAMS * STEPS,)),
            dma((CHUNKS,)),
            dma((CHUNKS + 1,)),
            dma((CHUNKS + 1,)),
            pltpu.SemaphoreType.REGULAR,
        ],
        compiler_params=pltpu.CompilerParams(
            collective_id=0, has_side_effects=True, vmem_limit_bytes=64 * 1024 * 1024 - 65536,
        ),
    )(amplitudes.transpose(2, 0, 1))


def solution(mesh):
    fine = Mesh(mesh.devices.reshape(2, 2, 4, 2, 4, 2), ("zb", "za", "y", "core", "x", "zh"))
    state, det = ("zb", "za", "y", "core"), ("x", "zh")
    return jax.shard_map(
        on_device,
        mesh=fine,
        in_specs=(P(state, det, None),),
        out_specs=P(None, state + det, None, None),
        check_vma=False,
    )
```

```python
import jax
import jax.numpy as jnp
from jax import lax
from jax.experimental import pallas as pl
from jax.experimental.pallas import tpu as pltpu
from jax.sharding import Mesh, PartitionSpec as P

MESH = pl.DeviceIdType.MESH
ROWS = 336
LANES = 384
SIZES = (96, 96, 80, 64)
STARTS = (0, 96, 192, 272)
CHUNKS = len(SIZES)
HOME, AWAY, NEAR = 0, CHUNKS, 2 * CHUNKS
STREAMS = 3 * CHUNKS
STEPS = 4


def group_of(a, scheme):
    if scheme == 0:
        return ((a + 1) // 2) % 2, a // 2
    return a // 2, a % 2


def product(left, right):
    return lax.dot_general(left, right, (((1,), (1,)), ((), ())), preferred_element_type=jnp.float32)


def lanes(rows):
    return lax.broadcasted_iota(jnp.int32, (rows, 128), 1)


def packed_rows(size):
    return 2 * size + size // 2 + 8


def pack(tile):
    size, third = tile.shape[0], tile[:, 256:]
    if third.shape[1] < 128:
        third = jnp.concatenate([third, jnp.zeros((size, 128 - third.shape[1]), jnp.float32)], 1)
    folded = jnp.where(lanes(size // 2) < 64, third[:size // 2], pltpu.roll(third[size // 2:], 64, 1))
    rest = jnp.concatenate([third, jnp.zeros((128 - size, 128), jnp.float32)], 0).T[64:72]
    return jnp.concatenate([tile[:, :128], tile[:, 128:256], folded, rest], 0)


def unpack(packed, size):
    end = packed_rows(size)
    folded = packed[2 * size:end - 8]
    third = jnp.concatenate([folded, pltpu.roll(folded, 64, 1)], 0)
    rest = jnp.concatenate([packed[end - 8:], jnp.zeros((120, 128), jnp.float32)], 0).T[:size]
    third = jnp.where(lanes(size) < 64, third, pltpu.roll(rest, 64, 1))
    return jnp.concatenate([packed[:size], packed[size:2 * size], third], 1)


def whole(chunks):
    return jnp.concatenate([unpack(chunk, size) for chunk, size in zip(chunks, SIZES)], 0)


def flipped(tile):
    return jnp.concatenate([tile, jnp.zeros((LANES - ROWS, LANES), jnp.float32)], 0).T


def remote(source, target, sends, recvs, send_at, recv_at, device):
    return pltpu.make_async_remote_copy(
        src_ref=source, dst_ref=target, send_sem=sends.at[send_at], recv_sem=recvs.at[recv_at],
        device_id=device, device_id_type=MESH,
    )


def by_state(raw, first, target, c):
    start, size = STARTS[c], SIZES[c]

    @pl.loop(0, target.shape[2] // 256)
    def _(i):
        part = pl.ds(pl.multiple_of(i * 256, 256), 256)
        target[:, start:start + size, part] = jnp.swapaxes(raw[first:first + size, :, part], 0, 1)


class Stream:
    def __init__(self, index, scheme, refs, sems):
        rows = pl.ds(0, packed_rows(SIZES[index % CHUNKS]))
        t, r1, r2, r3, f, r4 = refs
        self.t, self.r1 = t.at[index, :, :, :, rows], r1.at[index, :, :, rows]
        self.r2 = r2.at[index, :, rows]
        self.r3, self.f, self.r4 = (ref.at[index, rows] for ref in (r3, f, r4))
        self.sems, self.sem = sems, STEPS * index
        x, self.zh = lax.axis_index("x"), lax.axis_index("zh")
        self.group, self.member = group_of(x, scheme)
        near, far = {"x": x + 1 - 2 * (x % 2)}, {"x": 3 - x}
        self.first, self.second = (near, far) if scheme == 0 else (far, near)

    def copy(self, step, source, target, device):
        return remote(source, target, *self.sems, self.sem + step, self.sem + step, device)

    def over_x(self):
        self.copy0 = self.copy(0, self.t.at[1 - self.group], self.r1, self.first)
        self.copy0.start()

    def over_x_again(self):
        self.copy0.wait_recv()
        g, m = self.group, self.member
        self.t[g, 1 - m] += self.r1[1 - m]
        self.copy1 = self.copy(1, self.t.at[g, 1 - m], self.r2, self.second)
        self.copy1.start()
        self.t[g, m] += self.r1[m]

    def over_zh(self):
        self.copy1.wait_recv()
        g, m, h = self.group, self.member, self.zh
        self.t[g, m, 1 - h] += self.r2[1 - h]
        self.copy2 = self.copy(2, self.t.at[g, m, 1 - h], self.r3, {"zh": 1 - h})
        self.copy2.start()
        self.t[g, m, h] += self.r2[h]

    def summed(self):
        self.copy2.wait_recv()
        return self.t[self.group, self.member, self.zh] + self.r3[...]

    def to_mirror(self, value, device):
        self.f[...] = value
        self.copy3 = self.copy(3, self.f, self.r4, device)
        self.copy3.start()

    def go_home(self, r5, homes):
        self.copy1.wait_recv()
        g, m = self.group, self.member
        for bh in range(2):
            self.t[g, m, bh] += self.r2[bh]
        self.home_copies = [
            remote(self.t.at[g, m, bh], r5.at[self.zh], *self.sems, self.sem + 2 + bh, self.sem + 2 + self.zh, homes[bh])
            for bh in range(2)
        ]
        for copy in self.home_copies:
            copy.start()
        return [
            remote(self.t.at[g, m, z], r5.at[z], *self.sems, self.sem + 2 + z, self.sem + 2 + z, homes[z])
            for z in range(2)
        ]


def kernel(
    a_ref, out_ref, own, beside, held, raw_own, raw_beside, raw_held, t, r1, r2, r3, f, r4, r5,
    send_sem, recv_sem, load_sem, ex_send, ex_recv,
):
    zb, core = lax.axis_index("zb"), lax.axis_index("core")
    x, zh = lax.axis_index("x"), lax.axis_index("zh")
    half = held.shape[2]
    ops = out_ref.shape[1]

    other = {"zb": 1 - zb}
    home_mirror = {**other, "x": 2 * zh + (x + zb) % 2, "zh": x // 2}
    from_mirror = {**other, "x": 2 * zh + (x + 1 - zb) % 2, "zh": x // 2}
    homes = [{**other, "zh": z} for z in range(2)]
    near_mirror = {"core": 1 - core, "x": 2 * zh + (x + core) % 2, "zh": x // 2}
    partners = [
        {"core": 1 - core}, {"x": x + 1 - 2 * (x % 2)}, {"x": 3 - x}, {"zh": 1 - zh},
        *homes, home_mirror, from_mirror, near_mirror,
    ]
    barrier = pltpu.get_barrier_semaphore()
    for partner in partners:
        pl.semaphore_signal(barrier, inc=1, device_id=partner, device_id_type=MESH)
    pl.semaphore_wait(barrier, len(partners))

    here = pl.ds(pl.multiple_of(zb * half, half), half)
    away = pl.ds(pl.multiple_of((1 - zb) * half, half), half)
    valid = [min(size, ops - start) for start, size in zip(STARTS, SIZES)]
    exchange = []
    for c in range(CHUNKS):
        rows = pl.ds(STARTS[c], valid[c])
        exchange.append(remote(a_ref.at[rows, :, away], raw_held.at[rows], ex_send, ex_recv, c, c, other))
    for copy in exchange[:-1]:
        copy.start()
    to_side = remote(
        a_ref, raw_beside.at[pl.ds(0, ops)], ex_send, ex_recv, CHUNKS, CHUNKS, {"core": 1 - core}
    )
    to_side.start()
    loads = [
        pltpu.make_async_copy(
            a_ref.at[pl.ds(STARTS[c], valid[c])], raw_own.at[c % 2, pl.ds(0, valid[c])], load_sem.at[c]
        )
        for c in range(CHUNKS)
    ]
    loads[0].start()
    for c in range(CHUNKS):
        if c + 1 < CHUNKS:
            loads[c + 1].start()
        loads[c].wait()
        by_state(raw_own.at[c % 2], 0, own, c)

    refs, sems = (t, r1, r2, r3, f, r4), (send_sem, recv_sem)
    home = [Stream(HOME + c, 0, refs, sems) for c in range(CHUNKS)]
    going = [Stream(AWAY + c, 1, refs, sems) for c in range(CHUNKS)]
    near = [Stream(NEAR + c, c % 2, refs, sems) for c in range(CHUNKS)]

    to_side.wait_recv()
    for c in range(CHUNKS):
        by_state(raw_beside, STARTS[c], beside, c)

    @pl.loop(0, 4)
    def _(a):
        for bh in range(2):
            tile = product(beside[2 * bh + (a + core) % 2], own[a])
            for c in range(CHUNKS):
                g, m = group_of(a, c % 2)
                near[c].t[g, m, bh] = pack(tile[STARTS[c]:STARTS[c] + SIZES[c]])

    for stream in near:
        stream.over_x()
    for stream in near:
        stream.over_x_again()

    arrivals = []

    def far_chunk(c):
        exchange[c].wait_recv()
        by_state(raw_held, STARTS[c], held, c)
        rows, size = pl.ds(STARTS[c], SIZES[c]), SIZES[c]

        @pl.loop(0, 4)
        def _(a):
            left = [held[2 * bh + (a + role + zb) % 2, rows, :] for role in range(2) for bh in range(2)]
            tile = product(jnp.concatenate(left, 0), own[a, :, here])
            g, m = group_of(a, 0)
            for bh in range(2):
                home[c].t[g, m, bh] = pack(tile[bh * size:(bh + 1) * size])
                going[c].t[bh, (a + 1 + zb) % 2, a // 2] = pack(tile[(2 + bh) * size:(3 + bh) * size])

        home[c].over_x()
        going[c].over_x()
        if c == 0:
            for stream in near:
                stream.over_zh()
            exchange[-1].start()
        home[c].over_x_again()
        going[c].over_x_again()
        home[c].over_zh()
        arrivals.append(going[c].go_home(r5.at[c, :, pl.ds(0, packed_rows(size))], homes))

    for c in range(CHUNKS):
        far_chunk(c)

    for stream in near:
        stream.to_mirror(stream.summed(), near_mirror)
    slot = (x + core) % 2
    out_ref[1, :, slot] = flipped(whole([stream.f[...] for stream in near]))[:ops, :ops]

    for c in range(CHUNKS):
        for copy in arrivals[c]:
            copy.wait_recv()
    ends = [packed_rows(size) for size in SIZES]
    helped = flipped(whole([r5[c, 0, :ends[c]] + r5[c, 1, :ends[c]] for c in range(CHUNKS)]))
    for c in range(CHUNKS):
        part = helped[STARTS[c]:STARTS[c] + SIZES[c]]
        home[c].to_mirror(home[c].summed() + pack(part), home_mirror)
    for stream in near:
        stream.copy3.wait_recv()
    out_ref[1, :, 1 - slot] = whole([stream.r4[...] for stream in near])[:ops, :ops]
    slot = (x + zb) % 2
    out_ref[0, :, slot] = flipped(whole([stream.f[...] for stream in home]))[:ops, :ops]
    for c in range(CHUNKS):
        home[c].copy3.wait_recv()
        rows = pl.ds(STARTS[c], valid[c])
        out_ref[0, rows, 1 - slot] = unpack(home[c].r4[...], SIZES[c])[:valid[c], :ops]

    to_side.wait_send()
    for copy in exchange:
        copy.wait_send()
    for stream in (*home, *near):
        for copy in (stream.copy0, stream.copy1, stream.copy2, stream.copy3):
            copy.wait_send()
    for stream in going:
        for copy in (stream.copy0, stream.copy1, *stream.home_copies):
            copy.wait_send()


def on_device(amplitudes):
    states, dets, ops = amplitudes.shape
    dma = pltpu.SemaphoreType.DMA

    def tiles(*lead):
        return pltpu.VMEM((*lead, packed_rows(max(SIZES)), 128), jnp.float32)

    result = pl.pallas_call(
        kernel,
        out_shape=jax.ShapeDtypeStruct((2, ops, 2, ops), jnp.float32),
        in_specs=[pl.BlockSpec(memory_space=pl.ANY)],
        out_specs=pl.BlockSpec(memory_space=pltpu.VMEM),
        scratch_shapes=[
            pltpu.VMEM((states, ROWS, dets), jnp.bfloat16),
            pltpu.VMEM((states, ROWS, dets), jnp.bfloat16),
            pltpu.VMEM((states, ROWS, dets // 2), jnp.bfloat16),
            pltpu.VMEM((2, max(SIZES), states, dets), jnp.bfloat16),
            pltpu.VMEM((ROWS, states, dets), jnp.bfloat16),
            pltpu.VMEM((ROWS, states, dets // 2), jnp.bfloat16),
            tiles(STREAMS, 2, 2, 2),
            tiles(STREAMS, 2, 2),
            tiles(STREAMS, 2),
            tiles(STREAMS),
            tiles(STREAMS),
            tiles(STREAMS),
            tiles(CHUNKS, 2),
            dma((STREAMS * STEPS,)),
            dma((STREAMS * STEPS,)),
            dma((CHUNKS,)),
            dma((CHUNKS + 1,)),
            dma((CHUNKS + 1,)),
        ],
        compiler_params=pltpu.CompilerParams(
            collective_id=0, has_side_effects=True, vmem_limit_bytes=64 * 1024 * 1024 - 65536,
        ),
    )(amplitudes.transpose(2, 0, 1))
    return result.transpose(0, 2, 1, 3)


def solution(mesh):
    fine = Mesh(mesh.devices.reshape(2, 2, 4, 2, 4, 2), ("zb", "za", "y", "core", "x", "zh"))
    state, det = ("zb", "za", "y", "core"), ("x", "zh")
    return jax.shard_map(
        on_device,
        mesh=fine,
        in_specs=(P(state, det, None),),
        out_specs=P(None, state + det, None, None),
        check_vma=False,
    )
```

```python
import jax
import jax.numpy as jnp
from jax import lax
from jax.experimental import pallas as pl
from jax.experimental.pallas import tpu as pltpu
from jax.sharding import Mesh, PartitionSpec as P

MESH = pl.DeviceIdType.MESH
ROWS = 336
LANES = 384
SIZES = (96, 96, 80, 64)
STARTS = (0, 96, 192, 272)
KEPT = (96, 96, 80, 56)
CHUNKS = len(SIZES)
HOME, AWAY, NEAR = 0, CHUNKS, 2 * CHUNKS
STREAMS = 3 * CHUNKS
STEPS = 4


def group_of(a, scheme):
    if scheme == 0:
        return ((a + 1) // 2) % 2, a // 2
    return a // 2, a % 2


def product(left, right):
    return lax.dot_general(left, right, (((1,), (1,)), ((), ())), preferred_element_type=jnp.float32)


def lanes(rows):
    return lax.broadcasted_iota(jnp.int32, (rows, 128), 1)


def folded_rows(size):
    return (size + 15) // 16 * 8


def packed_rows(size):
    return 2 * size + folded_rows(size) + 8


def pack(tile):
    size, third = tile.shape[0], tile[:, 256:]
    if third.shape[1] < 128:
        third = jnp.concatenate([third, jnp.zeros((size, 128 - third.shape[1]), jnp.float32)], 1)
    fold = folded_rows(size)
    lower = third[fold:]
    if lower.shape[0] < fold:
        lower = jnp.concatenate([lower, jnp.zeros((fold - lower.shape[0], 128), jnp.float32)], 0)
    folded = jnp.where(lanes(fold) < 64, third[:fold], pltpu.roll(lower, 64, 1))
    rest = jnp.concatenate([third, jnp.zeros((128 - size, 128), jnp.float32)], 0).T[64:72]
    return jnp.concatenate([tile[:, :128], tile[:, 128:256], folded, rest], 0)


def unpack(packed, size):
    end = packed_rows(size)
    folded = packed[2 * size:end - 8]
    third = jnp.concatenate([folded, pltpu.roll(folded, 64, 1)[:size - folded.shape[0]]], 0)
    rest = jnp.concatenate([packed[end - 8:], jnp.zeros((120, 128), jnp.float32)], 0).T[:size]
    third = jnp.where(lanes(size) < 64, third, pltpu.roll(rest, 64, 1))
    return jnp.concatenate([packed[:size], packed[size:2 * size], third], 1)


def whole(chunks):
    return jnp.concatenate([unpack(chunk, size) for chunk, size in zip(chunks, KEPT)], 0)


def flipped(tile):
    return jnp.concatenate([tile, jnp.zeros((LANES - tile.shape[0], LANES), jnp.float32)], 0).T


def remote(source, target, sends, recvs, send_at, recv_at, device):
    return pltpu.make_async_remote_copy(
        src_ref=source, dst_ref=target, send_sem=sends.at[send_at], recv_sem=recvs.at[recv_at],
        device_id=device, device_id_type=MESH,
    )


def by_state(raw, first, target, c):
    start, size = STARTS[c], SIZES[c]

    @pl.loop(0, target.shape[2] // 256)
    def _(i):
        part = pl.ds(pl.multiple_of(i * 256, 256), 256)
        target[:, start:start + size, part] = jnp.swapaxes(raw[first:first + size, :, part], 0, 1)


class Stream:
    def __init__(self, index, scheme, refs, sems):
        rows = pl.ds(0, packed_rows(KEPT[index % CHUNKS]))
        t, r1, r2, r3, f, r4 = refs
        self.t, self.r1 = t.at[index, :, :, :, rows], r1.at[index, :, :, rows]
        self.r2 = r2.at[index, :, rows]
        self.r3, self.f, self.r4 = (ref.at[index, rows] for ref in (r3, f, r4))
        self.sems, self.sem = sems, STEPS * index
        x, self.zh = lax.axis_index("x"), lax.axis_index("zh")
        self.group, self.member = group_of(x, scheme)
        near, far = {"x": x + 1 - 2 * (x % 2)}, {"x": 3 - x}
        self.first, self.second = (near, far) if scheme == 0 else (far, near)

    def copy(self, step, source, target, device):
        return remote(source, target, *self.sems, self.sem + step, self.sem + step, device)

    def over_x(self):
        self.copy0 = self.copy(0, self.t.at[1 - self.group], self.r1, self.first)
        self.copy0.start()

    def over_x_again(self):
        self.copy0.wait_recv()
        g, m = self.group, self.member
        self.t[g, 1 - m] += self.r1[1 - m]
        self.copy1 = self.copy(1, self.t.at[g, 1 - m], self.r2, self.second)
        self.copy1.start()
        self.t[g, m] += self.r1[m]

    def over_zh(self):
        self.copy1.wait_recv()
        g, m, h = self.group, self.member, self.zh
        self.t[g, m, 1 - h] += self.r2[1 - h]
        self.copy2 = self.copy(2, self.t.at[g, m, 1 - h], self.r3, {"zh": 1 - h})
        self.copy2.start()
        self.t[g, m, h] += self.r2[h]

    def summed(self):
        self.copy2.wait_recv()
        return self.t[self.group, self.member, self.zh] + self.r3[...]

    def to_mirror(self, value, device):
        self.f[...] = value
        self.copy3 = self.copy(3, self.f, self.r4, device)
        self.copy3.start()

    def go_home(self, r5, homes):
        self.copy1.wait_recv()
        g, m = self.group, self.member
        for bh in range(2):
            self.t[g, m, bh] += self.r2[bh]
        self.home_copies = [
            remote(self.t.at[g, m, bh], r5.at[self.zh], *self.sems, self.sem + 2 + bh, self.sem + 2 + self.zh, homes[bh])
            for bh in range(2)
        ]
        for copy in self.home_copies:
            copy.start()
        return [
            remote(self.t.at[g, m, z], r5.at[z], *self.sems, self.sem + 2 + z, self.sem + 2 + z, homes[z])
            for z in range(2)
        ]


def kernel(
    a_ref, out_ref, own, beside, held, raw_own, raw_beside, raw_held, t, r1, r2, r3, f, r4, r5,
    send_sem, recv_sem, load_sem, ex_send, ex_recv,
):
    zb, core = lax.axis_index("zb"), lax.axis_index("core")
    x, zh = lax.axis_index("x"), lax.axis_index("zh")
    half = held.shape[2]
    ops = out_ref.shape[1]

    other = {"zb": 1 - zb}
    home_mirror = {**other, "x": 2 * zh + (x + zb) % 2, "zh": x // 2}
    from_mirror = {**other, "x": 2 * zh + (x + 1 - zb) % 2, "zh": x // 2}
    homes = [{**other, "zh": z} for z in range(2)]
    near_mirror = {"core": 1 - core, "x": 2 * zh + (x + core) % 2, "zh": x // 2}
    partners = [
        {"core": 1 - core}, {"x": x + 1 - 2 * (x % 2)}, {"x": 3 - x}, {"zh": 1 - zh},
        *homes, home_mirror, from_mirror, near_mirror,
    ]
    barrier = pltpu.get_barrier_semaphore()
    for partner in partners:
        pl.semaphore_signal(barrier, inc=1, device_id=partner, device_id_type=MESH)
    pl.semaphore_wait(barrier, len(partners))

    here = pl.ds(pl.multiple_of(zb * half, half), half)
    away = pl.ds(pl.multiple_of((1 - zb) * half, half), half)
    valid = [min(size, ops - start) for start, size in zip(STARTS, SIZES)]
    exchange = []
    for c in range(CHUNKS):
        rows = pl.ds(STARTS[c], valid[c])
        exchange.append(remote(a_ref.at[rows, :, away], raw_held.at[rows], ex_send, ex_recv, c, c, other))
    for copy in exchange:
        copy.start()
    to_side = remote(
        a_ref, raw_beside.at[pl.ds(0, ops)], ex_send, ex_recv, CHUNKS, CHUNKS, {"core": 1 - core}
    )
    to_side.start()
    loads = [
        pltpu.make_async_copy(
            a_ref.at[pl.ds(STARTS[c], valid[c])], raw_own.at[c % 2, pl.ds(0, valid[c])], load_sem.at[c]
        )
        for c in range(CHUNKS)
    ]
    loads[0].start()
    for c in range(CHUNKS):
        if c + 1 < CHUNKS:
            loads[c + 1].start()
        loads[c].wait()
        by_state(raw_own.at[c % 2], 0, own, c)

    refs, sems = (t, r1, r2, r3, f, r4), (send_sem, recv_sem)
    home = [Stream(HOME + c, 0, refs, sems) for c in range(CHUNKS)]
    going = [Stream(AWAY + c, 1, refs, sems) for c in range(CHUNKS)]
    near = [Stream(NEAR + c, c % 2, refs, sems) for c in range(CHUNKS)]

    to_side.wait_recv()
    for c in range(CHUNKS):
        by_state(raw_beside, STARTS[c], beside, c)

    @pl.loop(0, 4)
    def _(a):
        for bh in range(2):
            tile = product(beside[2 * bh + (a + core) % 2], own[a])
            for c in range(CHUNKS):
                g, m = group_of(a, c % 2)
                near[c].t[g, m, bh] = pack(tile[STARTS[c]:STARTS[c] + KEPT[c]])

    for stream in near:
        stream.over_x()
    for stream in near:
        stream.over_x_again()

    arrivals = []

    def far_chunk(c):
        exchange[c].wait_recv()
        by_state(raw_held, STARTS[c], held, c)
        rows, size = pl.ds(STARTS[c], SIZES[c]), SIZES[c]

        @pl.loop(0, 4)
        def _(a):
            left = [held[2 * bh + (a + role + zb) % 2, rows, :] for role in range(2) for bh in range(2)]
            tile = product(jnp.concatenate(left, 0), own[a, :, here])
            g, m = group_of(a, 0)
            for bh in range(2):
                home[c].t[g, m, bh] = pack(tile[bh * size:bh * size + KEPT[c]])
                going[c].t[bh, (a + 1 + zb) % 2, a // 2] = pack(tile[(2 + bh) * size:(2 + bh) * size + KEPT[c]])

        home[c].over_x()
        going[c].over_x()

    def again(c):
        home[c].over_x_again()
        going[c].over_x_again()

    def join(c):
        home[c].over_zh()
        arrivals.append(going[c].go_home(r5.at[c, :, pl.ds(0, packed_rows(KEPT[c]))], homes))

    for c in range(CHUNKS):
        far_chunk(c)
        if c + 1 == CHUNKS:
            for stream in near:
                stream.over_zh()
        if c >= 1:
            again(c - 1)
        if c >= 2:
            join(c - 2)
    again(CHUNKS - 1)
    join(CHUNKS - 2)
    join(CHUNKS - 1)

    for stream in near:
        stream.to_mirror(stream.summed(), near_mirror)
    slot = (x + core) % 2
    out_ref[1, :, slot] = flipped(whole([stream.f[...] for stream in near]))[:ops, :ops]

    for c in range(CHUNKS):
        for copy in arrivals[c]:
            copy.wait_recv()
    ends = [packed_rows(size) for size in KEPT]
    helped = flipped(whole([r5[c, 0, :ends[c]] + r5[c, 1, :ends[c]] for c in range(CHUNKS)]))
    for c in range(CHUNKS):
        part = helped[STARTS[c]:STARTS[c] + KEPT[c]]
        home[c].to_mirror(home[c].summed() + pack(part), home_mirror)
    for stream in near:
        stream.copy3.wait_recv()
    out_ref[1, :, 1 - slot] = whole([stream.r4[...] for stream in near])[:ops, :ops]
    slot = (x + zb) % 2
    out_ref[0, :, slot] = flipped(whole([stream.f[...] for stream in home]))[:ops, :ops]
    for c in range(CHUNKS):
        home[c].copy3.wait_recv()
        rows = pl.ds(STARTS[c], valid[c])
        out_ref[0, rows, 1 - slot] = unpack(home[c].r4[...], KEPT[c])[:valid[c], :ops]

    to_side.wait_send()
    for copy in exchange:
        copy.wait_send()
    for stream in (*home, *near):
        for copy in (stream.copy0, stream.copy1, stream.copy2, stream.copy3):
            copy.wait_send()
    for stream in going:
        for copy in (stream.copy0, stream.copy1, *stream.home_copies):
            copy.wait_send()


def on_device(amplitudes):
    states, dets, ops = amplitudes.shape
    dma = pltpu.SemaphoreType.DMA

    def tiles(*lead):
        return pltpu.VMEM((*lead, packed_rows(max(KEPT)), 128), jnp.float32)

    result = pl.pallas_call(
        kernel,
        out_shape=jax.ShapeDtypeStruct((2, ops, 2, ops), jnp.float32),
        in_specs=[pl.BlockSpec(memory_space=pl.ANY)],
        out_specs=pl.BlockSpec(memory_space=pltpu.VMEM),
        scratch_shapes=[
            pltpu.VMEM((states, ROWS, dets), jnp.bfloat16),
            pltpu.VMEM((states, ROWS, dets), jnp.bfloat16),
            pltpu.VMEM((states, ROWS, dets // 2), jnp.bfloat16),
            pltpu.VMEM((2, max(SIZES), states, dets), jnp.bfloat16),
            pltpu.VMEM((ROWS, states, dets), jnp.bfloat16),
            pltpu.VMEM((ROWS, states, dets // 2), jnp.bfloat16),
            tiles(STREAMS, 2, 2, 2),
            tiles(STREAMS, 2, 2),
            tiles(STREAMS, 2),
            tiles(STREAMS),
            tiles(STREAMS),
            tiles(STREAMS),
            tiles(CHUNKS, 2),
            dma((STREAMS * STEPS,)),
            dma((STREAMS * STEPS,)),
            dma((CHUNKS,)),
            dma((CHUNKS + 1,)),
            dma((CHUNKS + 1,)),
        ],
        compiler_params=pltpu.CompilerParams(
            collective_id=0, has_side_effects=True, vmem_limit_bytes=64 * 1024 * 1024 - 65536,
        ),
    )(amplitudes.transpose(2, 0, 1))
    return result.transpose(0, 2, 1, 3)


def solution(mesh):
    fine = Mesh(mesh.devices.reshape(2, 2, 4, 2, 4, 2), ("zb", "za", "y", "core", "x", "zh"))
    state, det = ("zb", "za", "y", "core"), ("x", "zh")
    return jax.shard_map(
        on_device,
        mesh=fine,
        in_specs=(P(state, det, None),),
        out_specs=P(None, state + det, None, None),
        check_vma=False,
    )
```

```python
import jax
import jax.numpy as jnp
from jax import lax
from jax.experimental import pallas as pl
from jax.experimental.pallas import tpu as pltpu
from jax.sharding import Mesh, PartitionSpec as P

MESH = pl.DeviceIdType.MESH
ROWS = 336
LANES = 384
SIZES = (112, 96, 80, 48)
STARTS = (0, 112, 208, 288)
KEPT = (112, 96, 80, 40)
CHUNKS = len(SIZES)
HOME, AWAY, NEAR = 0, CHUNKS, 2 * CHUNKS
STREAMS = 3 * CHUNKS
STEPS = 4


def group_of(a, scheme):
    if scheme == 0:
        return ((a + 1) // 2) % 2, a // 2
    return a // 2, a % 2


def product(left, right):
    return lax.dot_general(left, right, (((1,), (1,)), ((), ())), preferred_element_type=jnp.float32)


def lanes(rows):
    return lax.broadcasted_iota(jnp.int32, (rows, 128), 1)


def folded_rows(size):
    return (size + 15) // 16 * 8


def packed_rows(size):
    return 2 * size + folded_rows(size) + 8


def pack(tile):
    size, third = tile.shape[0], tile[:, 256:]
    if third.shape[1] < 128:
        third = jnp.concatenate([third, jnp.zeros((size, 128 - third.shape[1]), jnp.float32)], 1)
    fold = folded_rows(size)
    lower = third[fold:]
    if lower.shape[0] < fold:
        lower = jnp.concatenate([lower, jnp.zeros((fold - lower.shape[0], 128), jnp.float32)], 0)
    folded = jnp.where(lanes(fold) < 64, third[:fold], pltpu.roll(lower, 64, 1))
    rest = jnp.concatenate([third, jnp.zeros((128 - size, 128), jnp.float32)], 0).T[64:72]
    return jnp.concatenate([tile[:, :128], tile[:, 128:256], folded, rest], 0)


def unpack(packed, size):
    end = packed_rows(size)
    folded = packed[2 * size:end - 8]
    third = jnp.concatenate([folded, pltpu.roll(folded, 64, 1)[:size - folded.shape[0]]], 0)
    rest = jnp.concatenate([packed[end - 8:], jnp.zeros((120, 128), jnp.float32)], 0).T[:size]
    third = jnp.where(lanes(size) < 64, third, pltpu.roll(rest, 64, 1))
    return jnp.concatenate([packed[:size], packed[size:2 * size], third], 1)


def whole(chunks):
    return jnp.concatenate([unpack(chunk, size) for chunk, size in zip(chunks, KEPT)], 0)


def flipped(tile):
    return jnp.concatenate([tile, jnp.zeros((LANES - tile.shape[0], LANES), jnp.float32)], 0).T


def remote(source, target, sends, recvs, send_at, recv_at, device):
    return pltpu.make_async_remote_copy(
        src_ref=source, dst_ref=target, send_sem=sends.at[send_at], recv_sem=recvs.at[recv_at],
        device_id=device, device_id_type=MESH,
    )


def by_state(raw, first, target, c):
    start, size = STARTS[c], SIZES[c]

    @pl.loop(0, target.shape[2] // 256)
    def _(i):
        part = pl.ds(pl.multiple_of(i * 256, 256), 256)
        target[:, start:start + size, part] = jnp.swapaxes(raw[first:first + size, :, part], 0, 1)


class Stream:
    def __init__(self, index, scheme, refs, sems):
        rows = pl.ds(0, packed_rows(KEPT[index % CHUNKS]))
        t, r1, r2, r3, f, r4 = refs
        self.t, self.r1 = t.at[index, :, :, :, rows], r1.at[index, :, :, rows]
        self.r2 = r2.at[index, :, rows]
        self.r3, self.f, self.r4 = (ref.at[index, rows] for ref in (r3, f, r4))
        self.sems, self.sem = sems, STEPS * index
        x, self.zh = lax.axis_index("x"), lax.axis_index("zh")
        self.group, self.member = group_of(x, scheme)
        near, far = {"x": x + 1 - 2 * (x % 2)}, {"x": 3 - x}
        self.first, self.second = (near, far) if scheme == 0 else (far, near)

    def copy(self, step, source, target, device):
        return remote(source, target, *self.sems, self.sem + step, self.sem + step, device)

    def over_x(self):
        self.copy0 = self.copy(0, self.t.at[1 - self.group], self.r1, self.first)
        self.copy0.start()

    def over_x_again(self):
        self.copy0.wait_recv()
        g, m = self.group, self.member
        self.t[g, 1 - m] += self.r1[1 - m]
        self.copy1 = self.copy(1, self.t.at[g, 1 - m], self.r2, self.second)
        self.copy1.start()
        self.t[g, m] += self.r1[m]

    def over_zh(self):
        self.copy1.wait_recv()
        g, m, h = self.group, self.member, self.zh
        self.t[g, m, 1 - h] += self.r2[1 - h]
        self.copy2 = self.copy(2, self.t.at[g, m, 1 - h], self.r3, {"zh": 1 - h})
        self.copy2.start()
        self.t[g, m, h] += self.r2[h]

    def summed(self):
        self.copy2.wait_recv()
        return self.t[self.group, self.member, self.zh] + self.r3[...]

    def to_mirror(self, value, device):
        self.f[...] = value
        self.copy3 = self.copy(3, self.f, self.r4, device)
        self.copy3.start()

    def go_home(self, r5, homes):
        self.copy1.wait_recv()
        g, m = self.group, self.member
        for bh in range(2):
            self.t[g, m, bh] += self.r2[bh]
        self.home_copies = [
            remote(self.t.at[g, m, bh], r5.at[self.zh], *self.sems, self.sem + 2 + bh, self.sem + 2 + self.zh, homes[bh])
            for bh in range(2)
        ]
        for copy in self.home_copies:
            copy.start()
        return [
            remote(self.t.at[g, m, z], r5.at[z], *self.sems, self.sem + 2 + z, self.sem + 2 + z, homes[z])
            for z in range(2)
        ]


def kernel(
    a_ref, out_ref, own, beside, held, raw_own, raw_beside, raw_held, t, r1, r2, r3, f, r4, r5,
    send_sem, recv_sem, load_sem, ex_send, ex_recv,
):
    zb, core = lax.axis_index("zb"), lax.axis_index("core")
    x, zh = lax.axis_index("x"), lax.axis_index("zh")
    half = held.shape[2]
    ops = out_ref.shape[1]

    other = {"zb": 1 - zb}
    home_mirror = {**other, "x": 2 * zh + (x + zb) % 2, "zh": x // 2}
    from_mirror = {**other, "x": 2 * zh + (x + 1 - zb) % 2, "zh": x // 2}
    homes = [{**other, "zh": z} for z in range(2)]
    near_mirror = {"core": 1 - core, "x": 2 * zh + (x + core) % 2, "zh": x // 2}
    partners = [
        {"core": 1 - core}, {"x": x + 1 - 2 * (x % 2)}, {"x": 3 - x}, {"zh": 1 - zh},
        *homes, home_mirror, from_mirror, near_mirror,
    ]
    barrier = pltpu.get_barrier_semaphore()
    for partner in partners:
        pl.semaphore_signal(barrier, inc=1, device_id=partner, device_id_type=MESH)
    pl.semaphore_wait(barrier, len(partners))

    here = pl.ds(pl.multiple_of(zb * half, half), half)
    away = pl.ds(pl.multiple_of((1 - zb) * half, half), half)
    valid = [min(size, ops - start) for start, size in zip(STARTS, SIZES)]
    exchange = []
    for c in range(CHUNKS):
        rows = pl.ds(STARTS[c], valid[c])
        exchange.append(remote(a_ref.at[rows, :, away], raw_held.at[rows], ex_send, ex_recv, c, c, other))
    for copy in exchange:
        copy.start()
    to_side = remote(
        a_ref, raw_beside.at[pl.ds(0, ops)], ex_send, ex_recv, CHUNKS, CHUNKS, {"core": 1 - core}
    )
    to_side.start()
    loads = [
        pltpu.make_async_copy(
            a_ref.at[pl.ds(STARTS[c], valid[c])], raw_own.at[c % 2, pl.ds(0, valid[c])], load_sem.at[c]
        )
        for c in range(CHUNKS)
    ]
    loads[0].start()
    for c in range(CHUNKS):
        if c + 1 < CHUNKS:
            loads[c + 1].start()
        loads[c].wait()
        by_state(raw_own.at[c % 2], 0, own, c)

    refs, sems = (t, r1, r2, r3, f, r4), (send_sem, recv_sem)
    home = [Stream(HOME + c, 0, refs, sems) for c in range(CHUNKS)]
    going = [Stream(AWAY + c, 1, refs, sems) for c in range(CHUNKS)]
    near = [Stream(NEAR + c, c % 2, refs, sems) for c in range(CHUNKS)]

    to_side.wait_recv()
    for c in range(CHUNKS):
        by_state(raw_beside, STARTS[c], beside, c)

    @pl.loop(0, 4)
    def _(a):
        for bh in range(2):
            tile = product(beside[2 * bh + (a + core) % 2], own[a])
            for c in range(CHUNKS):
                g, m = group_of(a, c % 2)
                near[c].t[g, m, bh] = pack(tile[STARTS[c]:STARTS[c] + KEPT[c]])

    for stream in near:
        stream.over_x()
    for stream in near:
        stream.over_x_again()

    arrivals = []

    def far_chunk(c):
        exchange[c].wait_recv()
        by_state(raw_held, STARTS[c], held, c)
        rows, size = pl.ds(STARTS[c], SIZES[c]), SIZES[c]

        @pl.loop(0, 4)
        def _(a):
            left = [held[2 * bh + (a + role + zb) % 2, rows, :] for role in range(2) for bh in range(2)]
            tile = product(jnp.concatenate(left, 0), own[a, :, here])
            g, m = group_of(a, 0)
            for bh in range(2):
                home[c].t[g, m, bh] = pack(tile[bh * size:bh * size + KEPT[c]])
                going[c].t[bh, (a + 1 + zb) % 2, a // 2] = pack(tile[(2 + bh) * size:(2 + bh) * size + KEPT[c]])

        home[c].over_x()
        going[c].over_x()

    def again(c):
        home[c].over_x_again()
        going[c].over_x_again()

    def join(c):
        home[c].over_zh()
        arrivals.append(going[c].go_home(r5.at[c, :, pl.ds(0, packed_rows(KEPT[c]))], homes))

    for c in range(CHUNKS):
        far_chunk(c)
        if c + 1 == CHUNKS:
            for stream in near:
                stream.over_zh()
        if c >= 1:
            again(c - 1)
        if c >= 2:
            join(c - 2)
    again(CHUNKS - 1)
    join(CHUNKS - 2)
    join(CHUNKS - 1)

    for stream in near:
        stream.to_mirror(stream.summed(), near_mirror)
    slot = (x + core) % 2
    out_ref[1, :, slot] = flipped(whole([stream.f[...] for stream in near]))[:ops, :ops]

    for c in range(CHUNKS):
        for copy in arrivals[c]:
            copy.wait_recv()
    ends = [packed_rows(size) for size in KEPT]
    helped = flipped(whole([r5[c, 0, :ends[c]] + r5[c, 1, :ends[c]] for c in range(CHUNKS)]))
    for c in range(CHUNKS):
        part = helped[STARTS[c]:STARTS[c] + KEPT[c]]
        home[c].to_mirror(home[c].summed() + pack(part), home_mirror)
    for stream in near:
        stream.copy3.wait_recv()
    out_ref[1, :, 1 - slot] = whole([stream.r4[...] for stream in near])[:ops, :ops]
    slot = (x + zb) % 2
    out_ref[0, :, slot] = flipped(whole([stream.f[...] for stream in home]))[:ops, :ops]
    for c in range(CHUNKS):
        home[c].copy3.wait_recv()
        rows = pl.ds(STARTS[c], valid[c])
        out_ref[0, rows, 1 - slot] = unpack(home[c].r4[...], KEPT[c])[:valid[c], :ops]

    to_side.wait_send()
    for copy in exchange:
        copy.wait_send()
    for stream in (*home, *near):
        for copy in (stream.copy0, stream.copy1, stream.copy2, stream.copy3):
            copy.wait_send()
    for stream in going:
        for copy in (stream.copy0, stream.copy1, *stream.home_copies):
            copy.wait_send()


def on_device(amplitudes):
    states, dets, ops = amplitudes.shape
    dma = pltpu.SemaphoreType.DMA

    def tiles(*lead):
        return pltpu.VMEM((*lead, packed_rows(max(KEPT)), 128), jnp.float32)

    result = pl.pallas_call(
        kernel,
        out_shape=jax.ShapeDtypeStruct((2, ops, 2, ops), jnp.float32),
        in_specs=[pl.BlockSpec(memory_space=pl.ANY)],
        out_specs=pl.BlockSpec(memory_space=pltpu.VMEM),
        scratch_shapes=[
            pltpu.VMEM((states, ROWS, dets), jnp.bfloat16),
            pltpu.VMEM((states, ROWS, dets), jnp.bfloat16),
            pltpu.VMEM((states, ROWS, dets // 2), jnp.bfloat16),
            pltpu.VMEM((2, max(SIZES), states, dets), jnp.bfloat16),
            pltpu.VMEM((ROWS, states, dets), jnp.bfloat16),
            pltpu.VMEM((ROWS, states, dets // 2), jnp.bfloat16),
            tiles(STREAMS, 2, 2, 2),
            tiles(STREAMS, 2, 2),
            tiles(STREAMS, 2),
            tiles(STREAMS),
            tiles(STREAMS),
            tiles(STREAMS),
            tiles(CHUNKS, 2),
            dma((STREAMS * STEPS,)),
            dma((STREAMS * STEPS,)),
            dma((CHUNKS,)),
            dma((CHUNKS + 1,)),
            dma((CHUNKS + 1,)),
        ],
        compiler_params=pltpu.CompilerParams(
            collective_id=0, has_side_effects=True, vmem_limit_bytes=64 * 1024 * 1024 - 65536,
        ),
    )(amplitudes.transpose(2, 0, 1))
    return result.transpose(0, 2, 1, 3)


def solution(mesh):
    fine = Mesh(mesh.devices.reshape(2, 2, 4, 2, 4, 2), ("zb", "za", "y", "core", "x", "zh"))
    state, det = ("zb", "za", "y", "core"), ("x", "zh")
    return jax.shard_map(
        on_device,
        mesh=fine,
        in_specs=(P(state, det, None),),
        out_specs=P(None, state + det, None, None),
        check_vma=False,
    )
```
